128 devices in a mesh: dst: 64 (over x, z, y_lo, core), tok: 2 (over y_hi).
Axes of the slice: x: 4, y: 4 (y_hi: 2, y_lo: 2; y = y_hi * 2 + y_lo), z: 4, core: 2. Of those that a mesh axis runs over, the one named last changes fastest.
Arguments:
- latents: float32 [2048, 32768], P('tok', 'dst'), may hold values from 0 to 0.2, as said below
- mask: int32 [2048, 32768], P('tok', 'dst'), may hold values from 0 to 1
- errors: bfloat16 [2048, 4, 2048], P('tok'), may hold values from -6 to 6
- decoder: bfloat16 [32768, 4, 2048], P('dst'), may hold values from -0.125 to 0.125
Outputs:
- decoder_grad: bfloat16 [32768, 4, 2048], P('dst', None, 'tok')
- latent_grad: float32 [2048, 32768], P('tok', 'dst')
The draws below stay inside these ranges and needn't reach their ends.
Inputs may be any that keep to these rules, and one draw needn't show every extreme that they name: `latents`: zero exactly where mask is 0 and positive where mask is 1.
All inputs are finite; a program needn't handle non-finite values.
Results may differ from the reference program's by a relative error of at most 0.001.
Values may be sent and summed in bfloat16 or wider, within the bound.
No kernel may reach another device: no remote copies, remote signals or barrier semaphores. Data moves between devices by JAX's collectives and lax.ppermute only.
A program may use at most 192 MiB of HBM per device.

```python
import jax
import jax.numpy as jnp
from jax import lax

D = 2048
F = 8192
LAYERS = 4
TOKENS = 2048


def active_pattern(key):
    return jax.random.randint(jax.random.fold_in(key, 7), (TOKENS, LAYERS * F), 0, 2)


def draw_mask(key, part):
    return active_pattern(key).astype(jnp.int32)


def draw_latents(key, part):
    active = active_pattern(key).astype(jnp.float32)
    sub = jax.random.fold_in(key, 11)
    values = jax.random.uniform(sub, (TOKENS, LAYERS * F), jnp.float32, 0.02, 0.14)
    return active * values


def block_levels(own_key, shape, split, smallest, high):
    def one(position, shards_of):
        heights = jax.random.uniform(jax.random.fold_in(jax.random.fold_in(own_key, 6), position), (shards_of,), jnp.float32, smallest / len(split), high / len(split))
        return jnp.repeat(jnp.exp(heights), shape[position] // shards_of).reshape((-1,) + (1,) * (len(shape) - position - 1))

    factor_of = one(*split[0])
    for cut in split[1:]:
        factor_of = factor_of * one(*cut)
    return factor_of


def centred(rng, dims, scale, limit, pieces=(), held_as=jnp.bfloat16):
    values = scale * jax.random.normal(rng, dims, jnp.float32)
    if pieces:
        values = values * block_levels(rng, dims, pieces, -0.22, 0.18)
    return jnp.clip(values, -limit, limit).astype(held_as)


def setup_inputs(seed: int = 0) -> dict:
    key_list = jax.random.split(jax.random.key(seed), 5)
    latents = draw_latents(jax.random.fold_in(key_list[4], 71), 0)
    mask = draw_mask(jax.random.fold_in(key_list[4], 71), 0)
    errors = centred(key_list[2], (TOKENS, LAYERS, D), 1.0, 6.0, ((0, 2),))
    decoder = centred(key_list[3], (LAYERS * F, LAYERS, D), D ** -0.5, 0.125, ((0, 64),))
    return {"latents": latents, "mask": mask, "errors": errors, "decoder": decoder}


def reference(latents, mask, errors, decoder):
    grads = []
    latent_parts = [jnp.zeros((TOKENS, F), jnp.float32) for layer_index in range(LAYERS)]
    for target in range(LAYERS):
        errors_here = errors[:, target, :]
        errors_wide = errors_here.astype(jnp.float32)
        blocks = []
        for distance in range(LAYERS):
            if distance <= target:
                source = target - distance
                chosen = latents[:, source * F:(source + 1) * F]
                blocks.append(jnp.dot(chosen.T, errors_wide, precision=lax.Precision.HIGHEST, preferred_element_type=jnp.float32))
                weights = decoder[target * F:(target + 1) * F, distance, :]
                latent_parts[source] = latent_parts[source] + jnp.dot(errors_here, weights.T, preferred_element_type=jnp.float32)
            else:
                blocks.append(jnp.zeros((F, D), jnp.float32))
        grads.append(jnp.stack(blocks, axis=1).astype(jnp.bfloat16))
    decoder_grad = jnp.concatenate(grads, axis=0)
    latent_grad = mask.astype(jnp.float32) * jnp.concatenate(latent_parts, axis=1)
    return decoder_grad, latent_grad
```

```python
import jax
import jax.numpy as jnp
from jax import lax
from jax.experimental import pallas as pl
from jax.experimental.pallas import tpu as pltpu
from jax.sharding import PartitionSpec as P

LAYERS = 4
BF = jnp.bfloat16
F32 = jnp.float32
F16 = jnp.float16
LATENT_SCALE = 2.0**18
SUM_SCALE = 2.0**5


def params():
    return pltpu.CompilerParams(vmem_limit_bytes=60 << 20)


def cost(flops, moved):
    return pl.CostEstimate(flops=flops, bytes_accessed=moved, transcendentals=0)


def picker(tokens, layers):
    row = lax.broadcasted_iota(jnp.int32, (len(layers) * tokens, LAYERS * tokens), 0)
    col = lax.broadcasted_iota(jnp.int32, (len(layers) * tokens, LAYERS * tokens), 1)
    hit = None
    for i, layer in enumerate(layers):
        one = (row >= i * tokens) & (row < (i + 1) * tokens) & (col == (row - i * tokens) * LAYERS + layer)
        hit = one if hit is None else hit | one
    return hit.astype(F32).astype(BF)


def split_transposed(block):
    wide = block.T
    high = wide.astype(BF)
    low = (wide - high.astype(F32)).astype(BF)
    return jnp.concatenate([high, low], axis=1)


SUB = 128


def first_kernel(idx, er, lat, own_e, a_send, a_keep, o_send, o_keep, pick, e_a):
    step = pl.program_id(0)
    tokens, _, width = er.shape
    half = width // 2

    @pl.when(step == 0)
    def _():
        pick[...] = picker(SUB, [idx[0], idx[1]])

    for j in range(tokens // SUB):
        rows = er[j * SUB : (j + 1) * SUB].reshape(LAYERS * SUB, width)
        got = jnp.dot(pick[...], rows, preferred_element_type=F32).astype(BF)
        own_e[j * SUB : (j + 1) * SUB] = got[:SUB]
        e_a[j * SUB : (j + 1) * SUB] = got[SUB:]
    left = split_transposed(lat[...])
    keep = pl.multiple_of(idx[2] * half, half)
    send = pl.multiple_of((1 - idx[2]) * half, half)
    for out, source, start in ((a_send, e_a, send), (a_keep, e_a, keep), (o_send, own_e, send), (o_keep, own_e, keep)):
        right = source[:, pl.ds(start, half)]
        term = jnp.dot(left, jnp.concatenate([right, right], axis=0), preferred_element_type=F32)

        @pl.when(step == 0)
        def _():
            out[...] = term

        @pl.when(step > 0)
        def _():
            out[...] += term


def first_terms(idx, errors, latents):
    tokens, _, width = errors.shape
    f = latents.shape[1]
    half = width // 2
    tile = 256
    whole = pl.BlockSpec((f, half), lambda i, s: (0, 0))
    shape = jax.ShapeDtypeStruct((f, half), F32)
    return pl.pallas_call(
        first_kernel,
        name="first_terms",
        grid_spec=pltpu.PrefetchScalarGridSpec(
            num_scalar_prefetch=1,
            grid=(tokens // tile,),
            in_specs=[
                pl.BlockSpec((tile, LAYERS, width), lambda i, s: (i, 0, 0)),
                pl.BlockSpec((tile, f), lambda i, s: (i, 0)),
            ],
            out_specs=[pl.BlockSpec((tile, width), lambda i, s: (i, 0))] + [whole] * 4,
            scratch_shapes=[pltpu.VMEM((2 * SUB, LAYERS * SUB), BF), pltpu.VMEM((tile, width), BF)],
        ),
        out_shape=[jax.ShapeDtypeStruct((tokens, width), BF)] + [shape] * 4,
        compiler_params=params(),
        cost_estimate=cost(16 * tokens * f * width, 30 << 20),
    )(idx, errors, latents)


def more_kernel(idx, lat, e, send, keep, left):
    @pl.when(pl.program_id(0) == 0)
    def _():
        left[...] = split_transposed(lat[...])

    right = e[...]
    term = jnp.dot(left[...], jnp.concatenate([right, right], axis=0), preferred_element_type=F32)

    @pl.when(pl.program_id(0) < 2)
    def _():
        send[...] = term

    @pl.when(pl.program_id(0) >= 2)
    def _():
        keep[...] = term


def more_terms(idx, latents, e):
    tokens, f = latents.shape
    width = e.shape[1]
    tile = width // 4
    shape = jax.ShapeDtypeStruct((f, width // 2), F32)
    return pl.pallas_call(
        more_kernel,
        name="more_terms",
        grid_spec=pltpu.PrefetchScalarGridSpec(
            num_scalar_prefetch=1,
            grid=(4,),
            in_specs=[
                pl.BlockSpec((tokens, f), lambda i, s: (0, 0)),
                pl.BlockSpec((tokens, tile), lambda i, s: (0, lax.rem(i + 2 * (1 - s[2]), 4))),
            ],
            out_specs=[
                pl.BlockSpec((f, tile), lambda i, s: (0, jnp.minimum(i, 1))),
                pl.BlockSpec((f, tile), lambda i, s: (0, jnp.maximum(i - 2, 0))),
            ],
            scratch_shapes=[pltpu.VMEM((f, 2 * tokens), BF)],
        ),
        out_shape=[shape, shape],
        compiler_params=params(),
        cost_estimate=cost(4 * tokens * f * width, 12 << 20),
    )(idx, latents, e)


W_SUB = 64


def partial_kernel(e, w, own, others, pick, plain):
    f, _, width = w.shape

    @pl.when(pl.program_id(0) == 0)
    def _():
        pick[...] = picker(W_SUB, [0, 1, 2, 3])

    for j in range(f // W_SUB):
        rows = w[j * W_SUB : (j + 1) * W_SUB].reshape(LAYERS * W_SUB, width)
        got = jnp.dot(pick[...], rows, preferred_element_type=F32).astype(BF)
        for k in range(LAYERS):
            plain[k * f + j * W_SUB : k * f + (j + 1) * W_SUB] = got[k * W_SUB : (k + 1) * W_SUB]
    terms = lax.dot_general(e[...], plain[...], (((1,), (1,)), ((), ())), preferred_element_type=F32)
    own[...] = terms[:, :f]
    for k in range(1, LAYERS):
        others[k - 1] = terms[:, k * f : (k + 1) * f]


def partials(e, decoder):
    tokens, width = e.shape
    f = decoder.shape[0]
    tile = 128
    return pl.pallas_call(
        partial_kernel,
        name="partials",
        grid=(f // tile,),
        in_specs=[
            pl.BlockSpec((tokens, width), lambda i: (0, 0)),
            pl.BlockSpec((tile, LAYERS, width), lambda i: (i, 0, 0)),
        ],
        out_specs=[
            pl.BlockSpec((tokens, tile), lambda i: (0, i)),
            pl.BlockSpec((LAYERS - 1, tokens, tile), lambda i: (0, 0, i)),
        ],
        out_shape=[
            jax.ShapeDtypeStruct((tokens, f), F32),
            jax.ShapeDtypeStruct((LAYERS - 1, tokens, f), F32),
        ],
        scratch_shapes=[pltpu.VMEM((LAYERS * W_SUB, LAYERS * W_SUB), BF), pltpu.VMEM((LAYERS * tile, width), BF)],
        compiler_params=params(),
        cost_estimate=cost(8 * tokens * f * width, 20 << 20),
    )(e, decoder)


def weave_kernel(idx, own, slot_b, r_a, r_b, out, mix):
    f, width = own.shape
    place = idx[0]

    @pl.when(pl.program_id(0) == 0)
    def _():
        row = lax.broadcasted_iota(jnp.int32, (LAYERS * f, LAYERS * f), 0)
        col = lax.broadcasted_iota(jnp.int32, (LAYERS * f, LAYERS * f), 1)
        mix[...] = (col == (row % LAYERS) * f + row // LAYERS).astype(F32).astype(BF)

    zero = jnp.zeros((f, width), BF)
    one = jnp.where(place == 1, slot_b[...], jnp.where(place == 2, r_a[...], jnp.where(place == 3, r_b[...], zero)))
    two = jnp.where(place >= 2, slot_b[...], zero)
    three = jnp.where(place == 3, r_a[...], zero)
    rows = jnp.concatenate([own[...], one, two, three], axis=0)
    out[...] = jnp.dot(mix[...], rows, preferred_element_type=F32).astype(BF).reshape(f, LAYERS, width)


def weave(idx, own, slot_b, r_a, r_b):
    f, width = own.shape
    tile = 64
    block = pl.BlockSpec((tile, width), lambda i, s: (i, 0))
    return pl.pallas_call(
        weave_kernel,
        name="weave",
        grid_spec=pltpu.PrefetchScalarGridSpec(
            num_scalar_prefetch=1,
            grid=(f // tile,),
            in_specs=[block] * 4,
            out_specs=pl.BlockSpec((tile, LAYERS, width), lambda i, s: (i, 0, 0)),
            scratch_shapes=[pltpu.VMEM((LAYERS * tile, LAYERS * tile), BF)],
        ),
        out_shape=jax.ShapeDtypeStruct((f, LAYERS, width), BF),
        compiler_params=params(),
        cost_estimate=cost(2 * f * LAYERS * 256 * width, 8 << 20),
    )(idx, own, slot_b, r_a, r_b)


def moved(array, group, pairs):
    return lax.ppermute(array, "dst", [(a * group + i, b * group + i) for a, b in pairs for i in range(group)])


def swapped(array):
    return lax.ppermute((array * SUM_SCALE).astype(F16), "tok", [(0, 1), (1, 0)])


def joined(keep, arrived):
    return (keep + arrived.astype(F32) * (1 / SUM_SCALE)).astype(BF)


def per_device(latents, mask, errors, decoder):
    group = lax.axis_size("dst") // LAYERS
    place = lax.axis_index("dst") // group
    other = jnp.where(place == 1, 2, 3)
    idx = jnp.stack([place, other, lax.axis_index("tok")]).astype(jnp.int32)

    packed = (latents * LATENT_SCALE).astype(F16)
    from_near = moved(packed, group, [(0, 1), (1, 3)])
    from_far = moved(packed, group, [(0, 2)])

    own_e, a_send, a_keep, o_send, o_keep = first_terms(idx, errors, latents)
    a_come = swapped(a_send)
    o_come = swapped(o_send)

    own_p, other_p = partials(own_e, decoder)
    terms = [
        moved((other_p[k - 1] * SUM_SCALE).astype(F16), group, [(g, g - k) for g in range(k, LAYERS)])
        for k in range(1, LAYERS)
    ]

    foreign = (from_near.astype(F32) + from_far.astype(F32)) * (1 / LATENT_SCALE)
    b_send, b_keep = more_terms(idx, foreign, own_e)
    b_come = swapped(b_send)

    a_done = joined(a_keep, a_come)
    r_a = moved(a_done, group, [(0, 3), (1, 2)])
    r_b = moved(a_done, group, [(2, 3)])

    summed = own_p
    for term in terms:
        summed = summed + term.astype(F32) * (1 / SUM_SCALE)
    latent_grad = mask.astype(F32) * summed
    decoder_grad = weave(idx, joined(o_keep, o_come), joined(b_keep, b_come), r_a, r_b)
    return decoder_grad, latent_grad


def solution(mesh):
    placed = (P("tok", "dst"), P("tok", "dst"), P("tok", None, None), P("dst", None, None))
    return jax.shard_map(
        per_device,
        mesh=mesh,
        in_specs=placed,
        out_specs=(P("dst", None, "tok"), P("tok", "dst")),
        check_vma=False,
    )
```

```python
import jax
import jax.numpy as jnp
from jax import lax
from jax.experimental import pallas as pl
from jax.experimental.pallas import tpu as pltpu
from jax.sharding import PartitionSpec as P

LAYERS = 4
BF = jnp.bfloat16
F32 = jnp.float32
I16 = jnp.int16
SCALE_ROWS = 16


def params():
    return pltpu.CompilerParams(vmem_limit_bytes=60 << 20)


def cost(flops, moved):
    return pl.CostEstimate(flops=flops, bytes_accessed=moved, transcendentals=0)


def picker(tokens, layers):
    row = lax.broadcasted_iota(jnp.int32, (len(layers) * tokens, LAYERS * tokens), 0)
    col = lax.broadcasted_iota(jnp.int32, (len(layers) * tokens, LAYERS * tokens), 1)
    hit = None
    for i, layer in enumerate(layers):
        one = (row >= i * tokens) & (row < (i + 1) * tokens) & (col == (row - i * tokens) * LAYERS + layer)
        hit = one if hit is None else hit | one
    return hit.astype(F32).astype(BF)


def split_transposed(block):
    wide = block.T
    high = wide.astype(BF)
    low = (wide - high.astype(F32)).astype(BF)
    return jnp.concatenate([high, low], axis=1)


def encode(values, out):
    rows = values.shape[0]
    top = jnp.maximum(jnp.max(jnp.abs(values), axis=0, keepdims=True), 1e-30)
    power = jnp.ceil(jnp.log2(top))
    coded = jnp.clip(jnp.round(values * jnp.exp2(15 - power)), -32767, 32767)
    out[:rows] = coded.astype(jnp.int32).astype(I16)
    power = jnp.broadcast_to(power, (SCALE_ROWS, values.shape[1]))
    out[rows:] = power.astype(jnp.int32).astype(I16)


def wide(block):
    return block.astype(jnp.int32).astype(F32)


def unit(scales):
    return jnp.exp2(wide(scales)[:1] - 15)


SUB = 128


def first_kernel(idx, er, lat, own_e, a_code, a_keep, o_code, o_keep, pick, e_a, a_send, o_send):
    step = pl.program_id(0)
    tokens, _, width = er.shape
    half = width // 2

    @pl.when(step == 0)
    def _():
        pick[...] = picker(SUB, [idx[0], idx[1]])

    for j in range(tokens // SUB):
        rows = er[j * SUB : (j + 1) * SUB].reshape(LAYERS * SUB, width)
        got = jnp.dot(pick[...], rows, preferred_element_type=F32).astype(BF)
        own_e[j * SUB : (j + 1) * SUB] = got[:SUB]
        e_a[j * SUB : (j + 1) * SUB] = got[SUB:]
    left = split_transposed(lat[...])
    keep = pl.multiple_of(idx[2] * half, half)
    send = pl.multiple_of((1 - idx[2]) * half, half)
    for out, source, start in ((a_send, e_a, send), (a_keep, e_a, keep), (o_send, own_e, send), (o_keep, own_e, keep)):
        right = source[:, pl.ds(start, half)]
        term = jnp.dot(left, jnp.concatenate([right, right], axis=0), preferred_element_type=F32)
        out[...] = term + jnp.where(step > 0, out[...], 0.0)

    @pl.when(step == pl.num_programs(0) - 1)
    def _():
        encode(a_send[...], a_code)
        encode(o_send[...], o_code)


def first_terms(idx, errors, latents, tile=256):
    tokens, _, width = errors.shape
    f = latents.shape[1]
    half = width // 2
    whole = pl.BlockSpec((f, half), lambda i, s: (0, 0))
    whole_code = pl.BlockSpec((f + SCALE_ROWS, half), lambda i, s: (0, 0))
    shape = jax.ShapeDtypeStruct((f, half), F32)
    code = jax.ShapeDtypeStruct((f + SCALE_ROWS, half), I16)
    return pl.pallas_call(
        first_kernel,
        name="first_terms",
        grid_spec=pltpu.PrefetchScalarGridSpec(
            num_scalar_prefetch=1,
            grid=(tokens // tile,),
            in_specs=[
                pl.BlockSpec((tile, LAYERS, width), lambda i, s: (i, 0, 0)),
                pl.BlockSpec((tile, f), lambda i, s: (i, 0)),
            ],
            out_specs=[pl.BlockSpec((tile, width), lambda i, s: (i, 0)), whole_code, whole, whole_code, whole],
            scratch_shapes=[
                pltpu.VMEM((2 * SUB, LAYERS * SUB), BF),
                pltpu.VMEM((tile, width), BF),
                pltpu.VMEM((f, half), F32),
                pltpu.VMEM((f, half), F32),
            ],
        ),
        out_shape=[jax.ShapeDtypeStruct((tokens, width), BF), code, shape, code, shape],
        compiler_params=params(),
        cost_estimate=cost(16 * tokens * f * width, 30 << 20),
    )(idx, errors, latents)


def pack_kernel(lat, out):
    encode(lat[...], out)


def packed(latents):
    tokens, f = latents.shape
    tile = 256
    return pl.pallas_call(
        pack_kernel,
        name="pack",
        grid=(f // tile,),
        in_specs=[pl.BlockSpec((tokens, tile), lambda i: (0, i))],
        out_specs=pl.BlockSpec((tokens + SCALE_ROWS, tile), lambda i: (0, i)),
        out_shape=jax.ShapeDtypeStruct((tokens + SCALE_ROWS, f), I16),
        compiler_params=params(),
        cost_estimate=cost(tokens * f, 3 << 20),
    )(latents)


def more_kernel(idx, near, far, e, code, keep, left):
    step = pl.program_id(0)
    rows = near.shape[0] - SCALE_ROWS

    @pl.when(step == 0)
    def _():
        both = near[...].astype(jnp.int32) + far[...].astype(jnp.int32)
        left[...] = split_transposed(both[:rows].astype(F32) * jnp.exp2(both[rows : rows + 1].astype(F32) - 15))

    right = e[...]
    term = jnp.dot(left[...], jnp.concatenate([right, right], axis=0), preferred_element_type=F32)

    @pl.when(step < 2)
    def _():
        encode(term, code)

    @pl.when(step >= 2)
    def _():
        keep[...] = term


def more_terms(idx, near, far, e):
    rows, f = near.shape
    tokens, width = e.shape
    tile = width // 4
    half = width // 2
    return pl.pallas_call(
        more_kernel,
        name="more_terms",
        grid_spec=pltpu.PrefetchScalarGridSpec(
            num_scalar_prefetch=1,
            grid=(4,),
            in_specs=[
                pl.BlockSpec((rows, f), lambda i, s: (0, 0)),
                pl.BlockSpec((rows, f), lambda i, s: (0, 0)),
                pl.BlockSpec((tokens, tile), lambda i, s: (0, lax.rem(i + 2 * (1 - s[2]), 4))),
            ],
            out_specs=[
                pl.BlockSpec((f + SCALE_ROWS, tile), lambda i, s: (0, jnp.minimum(i, 1))),
                pl.BlockSpec((f, tile), lambda i, s: (0, jnp.maximum(i - 2, 0))),
            ],
            scratch_shapes=[pltpu.VMEM((f, 2 * tokens), BF)],
        ),
        out_shape=[jax.ShapeDtypeStruct((f + SCALE_ROWS, half), I16), jax.ShapeDtypeStruct((f, half), F32)],
        compiler_params=params(),
        cost_estimate=cost(4 * tokens * f * width, 12 << 20),
    )(idx, near, far, e)


def join_kernel(keep, come, scales, out):
    out[...] = (keep[...] + wide(come[...]) * unit(scales[...])).astype(BF)


def joined(keep, come):
    f, width = keep.shape
    tile = 128
    return pl.pallas_call(
        join_kernel,
        name="join",
        grid=(f // tile,),
        in_specs=[
            pl.BlockSpec((tile, width), lambda i: (i, 0)),
            pl.BlockSpec((tile, width), lambda i: (i, 0)),
            pl.BlockSpec((SCALE_ROWS, width), lambda i: (f // SCALE_ROWS, 0)),
        ],
        out_specs=pl.BlockSpec((tile, width), lambda i: (i, 0)),
        out_shape=jax.ShapeDtypeStruct((f, width), BF),
        compiler_params=params(),
        cost_estimate=cost(f * width, 4 << 20),
    )(keep, come, come)


W_SUB = 64


def partial_kernel(e, w, own, one, two, three, pick, plain):
    f, _, width = w.shape

    @pl.when(pl.program_id(0) == 0)
    def _():
        pick[...] = picker(W_SUB, [0, 1, 2, 3])

    for j in range(f // W_SUB):
        rows = w[j * W_SUB : (j + 1) * W_SUB].reshape(LAYERS * W_SUB, width)
        got = jnp.dot(pick[...], rows, preferred_element_type=F32).astype(BF)
        for k in range(LAYERS):
            plain[k * f + j * W_SUB : k * f + (j + 1) * W_SUB] = got[k * W_SUB : (k + 1) * W_SUB]
    terms = lax.dot_general(e[...], plain[...], (((1,), (1,)), ((), ())), preferred_element_type=F32)
    own[...] = terms[:, :f]
    for k, code in ((1, one), (2, two), (3, three)):
        encode(terms[:, k * f : (k + 1) * f], code)


def partials(e, decoder):
    tokens, width = e.shape
    f = decoder.shape[0]
    tile = 128
    return pl.pallas_call(
        partial_kernel,
        name="partials",
        grid=(f // tile,),
        in_specs=[
            pl.BlockSpec((tokens, width), lambda i: (0, 0)),
            pl.BlockSpec((tile, LAYERS, width), lambda i: (i, 0, 0)),
        ],
        out_specs=[
            pl.BlockSpec((tokens, tile), lambda i: (0, i)),
        ]
        + [pl.BlockSpec((tokens + SCALE_ROWS, tile), lambda i: (0, i))] * 3,
        out_shape=[jax.ShapeDtypeStruct((tokens, f), F32)] + [jax.ShapeDtypeStruct((tokens + SCALE_ROWS, f), I16)] * 3,
        scratch_shapes=[pltpu.VMEM((LAYERS * W_SUB, LAYERS * W_SUB), BF), pltpu.VMEM((LAYERS * tile, width), BF)],
        compiler_params=params(),
        cost_estimate=cost(8 * tokens * f * width, 20 << 20),
    )(e, decoder)


def weave_kernel(idx, o_keep, o_come, o_scale, b_keep, b_come, b_scale, r_a, r_b, out, mix):
    f, width = o_keep.shape
    place = idx[0]

    @pl.when(pl.program_id(0) == 0)
    def _():
        row = lax.broadcasted_iota(jnp.int32, (LAYERS * f, LAYERS * f), 0)
        col = lax.broadcasted_iota(jnp.int32, (LAYERS * f, LAYERS * f), 1)
        mix[...] = (col == (row % LAYERS) * f + row // LAYERS).astype(F32).astype(BF)

    own = (o_keep[...] + wide(o_come[...]) * unit(o_scale[...])).astype(BF)
    slot_b = (b_keep[...] + wide(b_come[...]) * unit(b_scale[...])).astype(BF)
    zero = jnp.zeros((f, width), BF)
    one = jnp.where(place == 1, slot_b, jnp.where(place == 2, r_a[...], jnp.where(place == 3, r_b[...], zero)))
    two = jnp.where(place >= 2, slot_b, zero)
    three = jnp.where(place == 3, r_a[...], zero)
    rows = jnp.concatenate([own, one, two, three], axis=0)
    out[...] = jnp.dot(mix[...], rows, preferred_element_type=F32).astype(BF).reshape(f, LAYERS, width)


def weave(idx, o_keep, o_come, b_keep, b_come, r_a, r_b):
    f, width = o_keep.shape
    tile = 64
    block = pl.BlockSpec((tile, width), lambda i, s: (i, 0))
    scale = pl.BlockSpec((SCALE_ROWS, width), lambda i, s: (f // SCALE_ROWS, 0))
    return pl.pallas_call(
        weave_kernel,
        name="weave",
        grid_spec=pltpu.PrefetchScalarGridSpec(
            num_scalar_prefetch=1,
            grid=(f // tile,),
            in_specs=[block, block, scale, block, block, scale, block, block],
            out_specs=pl.BlockSpec((tile, LAYERS, width), lambda i, s: (i, 0, 0)),
            scratch_shapes=[pltpu.VMEM((LAYERS * tile, LAYERS * tile), BF)],
        ),
        out_shape=jax.ShapeDtypeStruct((f, LAYERS, width), BF),
        compiler_params=params(),
        cost_estimate=cost(2 * f * LAYERS * 256 * width, 8 << 20),
    )(idx, o_keep, o_come, o_come, b_keep, b_come, b_come, r_a, r_b)


def moved(array, group, pairs):
    return lax.ppermute(array, "dst", [(a * group + i, b * group + i) for a, b in pairs for i in range(group)])


def swapped(array):
    return lax.ppermute(array, "tok", [(0, 1), (1, 0)])


def gate_kernel(mask, own, one, two, three, out):
    rows = own.shape[0]
    total = own[...]
    for code in (one, two, three):
        total = total + wide(code[:rows]) * unit(code[rows:])
    out[...] = mask[...].astype(F32) * total


def gated(mask, own, terms):
    tokens, f = own.shape
    tile = 128
    block = pl.BlockSpec((tokens, tile), lambda i: (0, i))
    return pl.pallas_call(
        gate_kernel,
        name="gate",
        grid=(f // tile,),
        in_specs=[block, block] + [pl.BlockSpec((tokens + SCALE_ROWS, tile), lambda i: (0, i))] * 3,
        out_specs=block,
        out_shape=jax.ShapeDtypeStruct((tokens, f), F32),
        compiler_params=params(),
        cost_estimate=cost(8 * tokens * f, 9 << 20),
    )(mask, own, *terms)


def per_device(latents, mask, errors, decoder):
    group = lax.axis_size("dst") // LAYERS
    place = lax.axis_index("dst") // group
    other = jnp.where(place == 1, 2, 3)
    idx = jnp.stack([place, other, lax.axis_index("tok")]).astype(jnp.int32)

    code = packed(latents)
    near = moved(code, group, [(0, 1), (1, 3)])
    far = moved(code, group, [(0, 2)])

    own_e, a_code, a_keep, o_code, o_keep = first_terms(idx, errors, latents)
    a_come = swapped(a_code)
    o_come = swapped(o_code)

    own_p, *other_p = partials(own_e, decoder)
    terms = [moved(other_p[k - 1], group, [(g, g - k) for g in range(k, LAYERS)]) for k in range(1, LAYERS)]

    b_code, b_keep = more_terms(idx, near, far, own_e)
    b_come = swapped(b_code)

    a_done = joined(a_keep, a_come)
    r_a = moved(a_done, group, [(0, 3), (1, 2)])
    r_b = moved(a_done, group, [(2, 3)])

    latent_grad = gated(mask, own_p, terms)
    decoder_grad = weave(idx, o_keep, o_come, b_keep, b_come, r_a, r_b)
    return decoder_grad, latent_grad


def solution(mesh):
    placed = (P("tok", "dst"), P("tok", "dst"), P("tok", None, None), P("dst", None, None))
    return jax.shard_map(
        per_device,
        mesh=mesh,
        in_specs=placed,
        out_specs=(P("dst", None, "tok"), P("tok", "dst")),
        check_vma=False,
    )
```

```python
import jax
import jax.numpy as jnp
from jax import lax
from jax.experimental import pallas as pl
from jax.experimental.pallas import tpu as pltpu
from jax.sharding import PartitionSpec as P


LAYERS = 4
BF = jnp.bfloat16
F32 = jnp.float32
I16 = jnp.int16
SCALE_ROWS = 16


def params():
    return pltpu.CompilerParams(vmem_limit_bytes=60 << 20)


def cost(flops, moved):
    return pl.CostEstimate(flops=flops, bytes_accessed=moved, transcendentals=0)


def picker(tokens, layers):
    row = lax.broadcasted_iota(jnp.int32, (len(layers) * tokens, LAYERS * tokens), 0)
    col = lax.broadcasted_iota(jnp.int32, (len(layers) * tokens, LAYERS * tokens), 1)
    hit = None
    for i, layer in enumerate(layers):
        one = (row >= i * tokens) & (row < (i + 1) * tokens) & (col == (row - i * tokens) * LAYERS + layer)
        hit = one if hit is None else hit | one
    return hit.astype(F32).astype(BF)


def split_transposed(block):
    wide = block.T
    high = wide.astype(BF)
    low = (wide - high.astype(F32)).astype(BF)
    return jnp.concatenate([high, low], axis=1)


def encode(values, out):
    rows = values.shape[0]
    top = jnp.maximum(jnp.max(jnp.abs(values), axis=0, keepdims=True), 1e-30)
    power = jnp.ceil(jnp.log2(top))
    coded = jnp.clip(jnp.round(values * jnp.exp2(15 - power)), -32767, 32767)
    out[:rows] = coded.astype(jnp.int32).astype(I16)
    power = jnp.broadcast_to(power, (SCALE_ROWS, values.shape[1]))
    out[rows:] = power.astype(jnp.int32).astype(I16)


def wide(block):
    return block.astype(jnp.int32).astype(F32)


def unit(scales):
    return jnp.exp2(wide(scales)[:1] - 15)


SUB = 64


def first_kernel(idx, er, lat, own_e, high, low, code, keep, pick, e_a, send):
    step = pl.program_id(0)
    tokens, _, width = er.shape
    half = width // 2

    @pl.when(step == 0)
    def _():
        pick[...] = picker(SUB, [idx[0], idx[1]])

    for j in range(tokens // SUB):
        rows = er[j * SUB : (j + 1) * SUB].reshape(LAYERS * SUB, width)
        got = jnp.dot(pick[...], rows, preferred_element_type=F32).astype(BF)
        own_e[j * SUB : (j + 1) * SUB] = got[:SUB]
        e_a[j * SUB : (j + 1) * SUB] = got[SUB:]
    left = split_transposed(lat[...])
    high[...] = left[:, :tokens]
    low[...] = left[:, tokens:]
    keep_at = pl.multiple_of(idx[2] * half, half)
    send_at = pl.multiple_of((1 - idx[2]) * half, half)

    @pl.when(idx[0] < LAYERS - 1)
    def _():
        for out, start in ((send, send_at), (keep, keep_at)):
            right = e_a[:, pl.ds(start, half)]
            term = jnp.dot(left, jnp.concatenate([right, right], axis=0), preferred_element_type=F32)
            out[...] = term + jnp.where(step > 0, out[...], 0.0)

    @pl.when((step == pl.num_programs(0) - 1) & (idx[0] < LAYERS - 1))
    def _():
        encode(send[...], code)


def first_terms(idx, errors, latents, tile=256):
    tokens, _, width = errors.shape
    f = latents.shape[1]
    half = width // 2
    return pl.pallas_call(
        first_kernel,
        name="first_terms",
        grid_spec=pltpu.PrefetchScalarGridSpec(
            num_scalar_prefetch=1,
            grid=(tokens // tile,),
            in_specs=[
                pl.BlockSpec((tile, LAYERS, width), lambda i, s: (i, 0, 0)),
                pl.BlockSpec((tile, f), lambda i, s: (i, 0)),
            ],
            out_specs=[
                pl.BlockSpec((tile, width), lambda i, s: (i, 0)),
                pl.BlockSpec((f, tile), lambda i, s: (0, i)),
                pl.BlockSpec((f, tile), lambda i, s: (0, i)),
                pl.BlockSpec((f + SCALE_ROWS, half), lambda i, s: (0, 0)),
                pl.BlockSpec((f, half), lambda i, s: (0, 0)),
            ],
            scratch_shapes=[
                pltpu.VMEM((2 * SUB, LAYERS * SUB), BF),
                pltpu.VMEM((tile, width), BF),
                pltpu.VMEM((f, half), F32),
            ],
        ),
        out_shape=[
            jax.ShapeDtypeStruct((tokens, width), BF),
            jax.ShapeDtypeStruct((f, tokens), BF),
            jax.ShapeDtypeStruct((f, tokens), BF),
            jax.ShapeDtypeStruct((f + SCALE_ROWS, half), I16),
            jax.ShapeDtypeStruct((f, half), F32),
        ],
        compiler_params=params(),
        cost_estimate=cost(8 * tokens * f * width, 30 << 20),
    )(idx, errors, latents)


def own_kernel(idx, high, low, e, code, keep):
    step = pl.program_id(0)

    def term():
        right = e[...]
        return jnp.dot(high[...], right, preferred_element_type=F32) + jnp.dot(low[...], right, preferred_element_type=F32)

    @pl.when(step < 2)
    def _():
        encode(term(), code)

    @pl.when(step >= 2)
    def _():
        keep[...] = term()


def own_terms(idx, high, low, e):
    f, tokens = high.shape
    width = e.shape[1]
    tile = width // 4
    half = width // 2
    return pl.pallas_call(
        own_kernel,
        name="own_terms",
        grid_spec=pltpu.PrefetchScalarGridSpec(
            num_scalar_prefetch=1,
            grid=(4,),
            in_specs=[
                pl.BlockSpec((f, tokens), lambda i, s: (0, 0)),
                pl.BlockSpec((f, tokens), lambda i, s: (0, 0)),
                pl.BlockSpec((tokens, tile), lambda i, s: (0, lax.rem(i + 2 * (1 - s[2]), 4))),
            ],
            out_specs=[
                pl.BlockSpec((f + SCALE_ROWS, tile), lambda i, s: (0, jnp.minimum(i, 1))),
                pl.BlockSpec((f, tile), lambda i, s: (0, jnp.maximum(i - 2, 0))),
            ],
        ),
        out_shape=[jax.ShapeDtypeStruct((f + SCALE_ROWS, half), I16), jax.ShapeDtypeStruct((f, half), F32)],
        compiler_params=params(),
        cost_estimate=cost(4 * tokens * f * width, 12 << 20),
    )(idx, high, low, e)


def pack_kernel(idx, lat, out):
    @pl.when(idx[0] < 2)
    def _():
        encode(lat[...], out)


def packed(idx, latents):
    tokens, f = latents.shape
    tile = 256
    return pl.pallas_call(
        pack_kernel,
        name="pack",
        grid_spec=pltpu.PrefetchScalarGridSpec(
            num_scalar_prefetch=1,
            grid=(f // tile,),
            in_specs=[pl.BlockSpec((tokens, tile), lambda i, s: (0, i))],
            out_specs=pl.BlockSpec((tokens + SCALE_ROWS, tile), lambda i, s: (0, i)),
        ),
        out_shape=jax.ShapeDtypeStruct((tokens + SCALE_ROWS, f), I16),
        compiler_params=params(),
        cost_estimate=cost(tokens * f, 3 << 20),
    )(idx, latents)


def more_kernel(idx, near, far, e, code, keep, left):
    step = pl.program_id(0)
    rows = near.shape[0] - SCALE_ROWS

    @pl.when((step == 0) & (idx[0] > 0))
    def _():
        both = near[...].astype(jnp.int32) + far[...].astype(jnp.int32)
        left[...] = split_transposed(both[:rows].astype(F32) * jnp.exp2(both[rows : rows + 1].astype(F32) - 15))

    def term():
        right = e[...]
        return jnp.dot(left[...], jnp.concatenate([right, right], axis=0), preferred_element_type=F32)

    @pl.when((step < 2) & (idx[0] > 0))
    def _():
        encode(term(), code)

    @pl.when((step >= 2) & (idx[0] > 0))
    def _():
        keep[...] = term()


def more_terms(idx, near, far, e):
    rows, f = near.shape
    tokens, width = e.shape
    tile = width // 4
    half = width // 2
    return pl.pallas_call(
        more_kernel,
        name="more_terms",
        grid_spec=pltpu.PrefetchScalarGridSpec(
            num_scalar_prefetch=1,
            grid=(4,),
            in_specs=[
                pl.BlockSpec((rows, f), lambda i, s: (0, 0)),
                pl.BlockSpec((rows, f), lambda i, s: (0, 0)),
                pl.BlockSpec((tokens, tile), lambda i, s: (0, lax.rem(i + 2 * (1 - s[2]), 4))),
            ],
            out_specs=[
                pl.BlockSpec((f + SCALE_ROWS, tile), lambda i, s: (0, jnp.minimum(i, 1))),
                pl.BlockSpec((f, tile), lambda i, s: (0, jnp.maximum(i - 2, 0))),
            ],
            scratch_shapes=[pltpu.VMEM((f, 2 * tokens), BF)],
        ),
        out_shape=[jax.ShapeDtypeStruct((f + SCALE_ROWS, half), I16), jax.ShapeDtypeStruct((f, half), F32)],
        compiler_params=params(),
        cost_estimate=cost(4 * tokens * f * width, 12 << 20),
    )(idx, near, far, e)


def join_kernel(keep, come, scales, out):
    out[...] = (keep[...] + wide(come[...]) * unit(scales[...])).astype(BF)


def joined(keep, come):
    f, width = keep.shape
    tile = 256
    return pl.pallas_call(
        join_kernel,
        name="join",
        grid=(f // tile,),
        in_specs=[
            pl.BlockSpec((tile, width), lambda i: (i, 0)),
            pl.BlockSpec((tile, width), lambda i: (i, 0)),
            pl.BlockSpec((SCALE_ROWS, width), lambda i: (f // SCALE_ROWS, 0)),
        ],
        out_specs=pl.BlockSpec((tile, width), lambda i: (i, 0)),
        out_shape=jax.ShapeDtypeStruct((f, width), BF),
        compiler_params=params(),
        cost_estimate=cost(f * width, 4 << 20),
    )(keep, come, come)


W_SUB = 64


def far_kernel(idx, e, w, zero, one, two, three, pick, plain):
    f, _, width = w.shape

    @pl.when(pl.program_id(0) == 0)
    def _():
        pick[...] = picker(W_SUB, [0, 1, 2, 3])

    for j in range(f // W_SUB):
        rows = w[j * W_SUB : (j + 1) * W_SUB].reshape(LAYERS * W_SUB, width)
        got = jnp.dot(pick[...], rows, preferred_element_type=F32).astype(BF)
        part = slice(j * W_SUB, (j + 1) * W_SUB)
        zero[part] = got[:W_SUB]
        one[part] = got[W_SUB : 2 * W_SUB]
        plain[j * W_SUB : (j + 1) * W_SUB] = got[2 * W_SUB : 3 * W_SUB]
        plain[f + j * W_SUB : f + (j + 1) * W_SUB] = got[3 * W_SUB :]
    dims = (((1,), (1,)), ((), ()))

    @pl.when(idx[0] == 2)
    def _():
        encode(lax.dot_general(e[...], plain[:f], dims, preferred_element_type=F32), two)

    @pl.when(idx[0] == 3)
    def _():
        terms = lax.dot_general(e[...], plain[...], dims, preferred_element_type=F32)
        encode(terms[:, :f], two)
        encode(terms[:, f:], three)


def far_partials(idx, e, decoder):
    tokens, width = e.shape
    f = decoder.shape[0]
    tile = 128
    weights = pl.BlockSpec((tile, width), lambda i, s: (i, 0))
    code = pl.BlockSpec((tokens + SCALE_ROWS, tile), lambda i, s: (0, i))
    return pl.pallas_call(
        far_kernel,
        name="far_partials",
        grid_spec=pltpu.PrefetchScalarGridSpec(
            num_scalar_prefetch=1,
            grid=(f // tile,),
            in_specs=[
                pl.BlockSpec((tokens, width), lambda i, s: (0, 0)),
                pl.BlockSpec((tile, LAYERS, width), lambda i, s: (i, 0, 0)),
            ],
            out_specs=[weights, weights, code, code],
            scratch_shapes=[pltpu.VMEM((LAYERS * W_SUB, LAYERS * W_SUB), BF), pltpu.VMEM((2 * tile, width), BF)],
        ),
        out_shape=[jax.ShapeDtypeStruct((f, width), BF)] * 2 + [jax.ShapeDtypeStruct((tokens + SCALE_ROWS, f), I16)] * 2,
        compiler_params=params(),
        cost_estimate=cost(4 * tokens * f * width, 20 << 20),
    )(idx, e, decoder)


def near_kernel(idx, e, zero, one, own, code):
    dims = (((1,), (1,)), ((), ()))

    @pl.when(idx[0] > 0)
    def _():
        encode(lax.dot_general(e[...], one[...], dims, preferred_element_type=F32), code)

    own[...] = lax.dot_general(e[...], zero[...], dims, preferred_element_type=F32)


def near_partials(idx, e, zero, one):
    tokens, width = e.shape
    f = zero.shape[0]
    tile = 256
    weights = pl.BlockSpec((tile, width), lambda i, s: (i, 0))
    return pl.pallas_call(
        near_kernel,
        name="near_partials",
        grid_spec=pltpu.PrefetchScalarGridSpec(
            num_scalar_prefetch=1,
            grid=(f // tile,),
            in_specs=[pl.BlockSpec((tokens, width), lambda i, s: (0, 0)), weights, weights],
            out_specs=[
                pl.BlockSpec((tokens, tile), lambda i, s: (0, i)),
                pl.BlockSpec((tokens + SCALE_ROWS, tile), lambda i, s: (0, i)),
            ],
        ),
        out_shape=[jax.ShapeDtypeStruct((tokens, f), F32), jax.ShapeDtypeStruct((tokens + SCALE_ROWS, f), I16)],
        compiler_params=params(),
        cost_estimate=cost(4 * tokens * f * width, 12 << 20),
    )(idx, e, zero, one)


def weave_kernel(idx, o_keep, o_come, o_scale, b_keep, b_come, b_scale, r_a, r_b, out, mix):
    f, width = o_keep.shape
    place = idx[0]

    @pl.when(pl.program_id(0) == 0)
    def _():
        row = lax.broadcasted_iota(jnp.int32, (LAYERS * f, LAYERS * f), 0)
        col = lax.broadcasted_iota(jnp.int32, (LAYERS * f, LAYERS * f), 1)
        mix[...] = (col == (row % LAYERS) * f + row // LAYERS).astype(F32).astype(BF)

    own = (o_keep[...] + wide(o_come[...]) * unit(o_scale[...])).astype(BF)
    slot_b = (b_keep[...] + wide(b_come[...]) * unit(b_scale[...])).astype(BF)
    zero = jnp.zeros((f, width), BF)
    one = jnp.where(place == 0, zero, jnp.where(place == 3, r_b[...], slot_b))
    two = jnp.where(place >= 2, r_a[...], zero)
    three = jnp.where(place == 3, slot_b, zero)
    rows = jnp.concatenate([own, one, two, three], axis=0)
    out[...] = jnp.dot(mix[...], rows, preferred_element_type=F32).astype(BF).reshape(f, LAYERS, width)


def weave(idx, o_keep, o_come, b_keep, b_come, r_a, r_b):
    f, width = o_keep.shape
    tile = 64
    block = pl.BlockSpec((tile, width), lambda i, s: (i, 0))
    scale = pl.BlockSpec((SCALE_ROWS, width), lambda i, s: (f // SCALE_ROWS, 0))
    return pl.pallas_call(
        weave_kernel,
        name="weave",
        grid_spec=pltpu.PrefetchScalarGridSpec(
            num_scalar_prefetch=1,
            grid=(f // tile,),
            in_specs=[block, block, scale, block, block, scale, block, block],
            out_specs=pl.BlockSpec((tile, LAYERS, width), lambda i, s: (i, 0, 0)),
            scratch_shapes=[pltpu.VMEM((LAYERS * tile, LAYERS * tile), BF)],
        ),
        out_shape=jax.ShapeDtypeStruct((f, LAYERS, width), BF),
        compiler_params=params(),
        cost_estimate=cost(2 * f * LAYERS * 256 * width, 8 << 20),
    )(idx, o_keep, o_come, o_come, b_keep, b_come, b_come, r_a, r_b)


def moved(array, group, pairs):
    return lax.ppermute(array, "dst", [(a * group + i, b * group + i) for a, b in pairs for i in range(group)])


def swapped(array):
    return lax.ppermute(array, "tok", [(0, 1), (1, 0)])


def gate_kernel(mask, own, one, two, three, out):
    rows = own.shape[0]
    total = own[...]
    for code in (one, two, three):
        total = total + wide(code[:rows]) * unit(code[rows:])
    out[...] = mask[...].astype(F32) * total


def gated(mask, own, terms):
    tokens, f = own.shape
    tile = 128
    block = pl.BlockSpec((tokens, tile), lambda i: (0, i))
    return pl.pallas_call(
        gate_kernel,
        name="gate",
        grid=(f // tile,),
        in_specs=[block, block] + [pl.BlockSpec((tokens + SCALE_ROWS, tile), lambda i: (0, i))] * 3,
        out_specs=block,
        out_shape=jax.ShapeDtypeStruct((tokens, f), F32),
        compiler_params=params(),
        cost_estimate=cost(8 * tokens * f, 9 << 20),
    )(mask, own, *terms)


def after(array, earlier):
    return lax.optimization_barrier((array, earlier))[0]


def per_device(latents, mask, errors, decoder):
    group = lax.axis_size("dst") // LAYERS
    place = lax.axis_index("dst") // group
    other = jnp.where(place == 0, 2, 3)
    idx = jnp.stack([place, other, lax.axis_index("tok")]).astype(jnp.int32)

    own_e, high, low, a_code, a_keep = first_terms(idx, errors, latents)
    a_come = swapped(a_code)

    code = packed(idx, after(latents, a_code))
    near = moved(code, group, [(0, 1), (1, 2)])
    far = moved(code, group, [(0, 3)])

    zero, one, two_p, three_p = far_partials(idx, after(own_e, code), decoder)
    three = moved(three_p, group, [(3, 0)])
    two = moved(two_p, group, [(3, 1), (2, 0)])

    o_code, o_keep = own_terms(idx, after(high, two_p), low, own_e)
    o_come = swapped(o_code)

    a_done = joined(after(a_keep, o_code), a_come)
    r_a = moved(a_done, group, [(0, 2), (1, 3)])
    r_b = moved(a_done, group, [(2, 3)])

    own_p, one_p = near_partials(idx, after(own_e, a_done), zero, one)
    one = moved(one_p, group, [(3, 2), (2, 1), (1, 0)])

    b_code, b_keep = more_terms(idx, after(near, one_p), far, own_e)
    b_come = swapped(b_code)

    latent_grad = gated(after(mask, b_code), own_p, (one, two, three))
    decoder_grad = weave(idx, after(o_keep, latent_grad), o_come, b_keep, b_come, r_a, r_b)
    return decoder_grad, latent_grad


def solution(mesh):
    placed = (P("tok", "dst"), P("tok", "dst"), P("tok", None, None), P("dst", None, None))
    return jax.shard_map(
        per_device,
        mesh=mesh,
        in_specs=placed,
        out_specs=(P("dst", None, "tok"), P("tok", "dst")),
        check_vma=False,
    )
```

```python
import jax
import jax.numpy as jnp
from jax import lax
from jax.experimental import pallas as pl
from jax.experimental.pallas import tpu as pltpu
from jax.sharding import PartitionSpec as P


LAYERS = 4
BF = jnp.bfloat16
F32 = jnp.float32
I16 = jnp.int16
SCALE_ROWS = 16


def params(mib=60):
    return pltpu.CompilerParams(vmem_limit_bytes=mib << 20)


def cost(flops, moved):
    return pl.CostEstimate(flops=flops, bytes_accessed=moved, transcendentals=0)


def picker(tokens, layers):
    row = lax.broadcasted_iota(jnp.int32, (len(layers) * tokens, LAYERS * tokens), 0)
    col = lax.broadcasted_iota(jnp.int32, (len(layers) * tokens, LAYERS * tokens), 1)
    hit = None
    for i, layer in enumerate(layers):
        one = (row >= i * tokens) & (row < (i + 1) * tokens) & (col == (row - i * tokens) * LAYERS + layer)
        hit = one if hit is None else hit | one
    return hit.astype(F32).astype(BF)


def split_transposed(block):
    wide = block.T
    high = wide.astype(BF)
    low = (wide - high.astype(F32)).astype(BF)
    return jnp.concatenate([high, low], axis=1)


def encode(values, out):
    rows = values.shape[0]
    top = jnp.maximum(jnp.max(jnp.abs(values), axis=0, keepdims=True), 1e-30)
    power = jnp.ceil(jnp.log2(top))
    coded = jnp.clip(jnp.round(values * jnp.exp2(15 - power)), -32767, 32767)
    out[:rows] = coded.astype(jnp.int32).astype(I16)
    power = jnp.broadcast_to(power, (SCALE_ROWS, values.shape[1]))
    out[rows:] = power.astype(jnp.int32).astype(I16)


def wide(block):
    return block.astype(jnp.int32).astype(F32)


def unit(scales):
    return jnp.exp2(wide(scales)[:1] - 15)


SUB = 64


def first_kernel(idx, er, lat, own_e, l_code, a_code, a_keep, o_code, o_keep, pick, e_a, a_send, o_send):
    step = pl.program_id(0)
    tokens, _, width = er.shape
    half = width // 2
    last = step == pl.num_programs(0) - 1
    early = idx[0] < LAYERS - 1

    @pl.when(step == 0)
    def _():
        pick[...] = picker(SUB, [idx[0], idx[1]])

    for j in range(tokens // SUB):
        rows = er[j * SUB : (j + 1) * SUB].reshape(LAYERS * SUB, width)
        got = jnp.dot(pick[...], rows, preferred_element_type=F32).astype(BF)
        own_e[j * SUB : (j + 1) * SUB] = got[:SUB]
        e_a[j * SUB : (j + 1) * SUB] = got[SUB:]
    left = split_transposed(lat[pl.ds(pl.multiple_of(step * tokens, tokens), tokens)])
    keep_at = pl.multiple_of(idx[2] * half, half)
    send_at = pl.multiple_of((1 - idx[2]) * half, half)

    def add(out, source, start):
        right = source[:, pl.ds(start, half)]
        term = jnp.dot(left, jnp.concatenate([right, right], axis=0), preferred_element_type=F32)
        out[...] = term + jnp.where(step > 0, out[...], 0.0)

    add(o_send, own_e, send_at)
    add(o_keep, own_e, keep_at)

    @pl.when(early)
    def _():
        add(a_send, e_a, send_at)
        add(a_keep, e_a, keep_at)

    @pl.when(last & early)
    def _():
        encode(a_send[...], a_code)

    @pl.when(last)
    def _():
        encode(o_send[...], o_code)

    @pl.when(last & (idx[0] < 2))
    def _():
        encode(lat[...], l_code)


def first_terms(idx, errors, latents, tile=256):
    tokens, _, width = errors.shape
    f = latents.shape[1]
    half = width // 2
    whole = pl.BlockSpec((f, half), lambda i, s: (0, 0))
    whole_code = pl.BlockSpec((f + SCALE_ROWS, half), lambda i, s: (0, 0))
    shape = jax.ShapeDtypeStruct((f, half), F32)
    code = jax.ShapeDtypeStruct((f + SCALE_ROWS, half), I16)
    return pl.pallas_call(
        first_kernel,
        name="first_terms",
        grid_spec=pltpu.PrefetchScalarGridSpec(
            num_scalar_prefetch=1,
            grid=(tokens // tile,),
            in_specs=[
                pl.BlockSpec((tile, LAYERS, width), lambda i, s: (i, 0, 0)),
                pl.BlockSpec((tokens, f), lambda i, s: (0, 0)),
            ],
            out_specs=[
                pl.BlockSpec((tile, width), lambda i, s: (i, 0)),
                pl.BlockSpec((tokens + SCALE_ROWS, f), lambda i, s: (0, 0)),
                whole_code,
                whole,
                whole_code,
                whole,
            ],
            scratch_shapes=[
                pltpu.VMEM((2 * SUB, LAYERS * SUB), BF),
                pltpu.VMEM((tile, width), BF),
                pltpu.VMEM((f, half), F32),
                pltpu.VMEM((f, half), F32),
            ],
        ),
        out_shape=[
            jax.ShapeDtypeStruct((tokens, width), BF),
            jax.ShapeDtypeStruct((tokens + SCALE_ROWS, f), I16),
            code,
            shape,
            code,
            shape,
        ],
        compiler_params=params(),
        cost_estimate=cost(16 * tokens * f * width, 30 << 20),
    )(idx, errors, latents)


def more_kernel(idx, near, far, e, a_keep, a_come, a_scale, a_done, code, keep, left):
    step = pl.program_id(0)
    rows = near.shape[0] - SCALE_ROWS
    late = idx[0] > 0
    a_done[...] = (a_keep[...] + wide(a_come[...]) * unit(a_scale[...])).astype(BF)

    @pl.when((step == 0) & late)
    def _():
        both = near[...].astype(jnp.int32) + far[...].astype(jnp.int32)
        left[...] = split_transposed(both[:rows].astype(F32) * jnp.exp2(both[rows : rows + 1].astype(F32) - 15))

    def term():
        right = e[...]
        return jnp.dot(left[...], jnp.concatenate([right, right], axis=0), preferred_element_type=F32)

    @pl.when((step < 2) & late)
    def _():
        encode(term(), code)

    @pl.when((step >= 2) & late)
    def _():
        keep[...] = term()


def more_terms(idx, near, far, e, a_keep, a_come):
    rows, f = near.shape
    tokens, width = e.shape
    tile = width // 4
    half = width // 2
    part = pl.BlockSpec((f // 4, half), lambda i, s: (i, 0))
    return pl.pallas_call(
        more_kernel,
        name="more_terms",
        grid_spec=pltpu.PrefetchScalarGridSpec(
            num_scalar_prefetch=1,
            grid=(4,),
            in_specs=[
                pl.BlockSpec((rows, f), lambda i, s: (0, 0)),
                pl.BlockSpec((rows, f), lambda i, s: (0, 0)),
                pl.BlockSpec((tokens, tile), lambda i, s: (0, lax.rem(i + 2 * (1 - s[2]), 4))),
                part,
                part,
                pl.BlockSpec((SCALE_ROWS, half), lambda i, s: (f // SCALE_ROWS, 0)),
            ],
            out_specs=[
                part,
                pl.BlockSpec((f + SCALE_ROWS, tile), lambda i, s: (0, jnp.minimum(i, 1))),
                pl.BlockSpec((f, tile), lambda i, s: (0, jnp.maximum(i - 2, 0))),
            ],
            scratch_shapes=[pltpu.VMEM((f, 2 * tokens), BF)],
        ),
        out_shape=[
            jax.ShapeDtypeStruct((f, half), BF),
            jax.ShapeDtypeStruct((f + SCALE_ROWS, half), I16),
            jax.ShapeDtypeStruct((f, half), F32),
        ],
        compiler_params=params(40),
        cost_estimate=cost(4 * tokens * f * width, 12 << 20),
    )(idx, near, far, e, a_keep, a_come, a_come)


W_SUB = 64


def partial_kernel(idx, e, w, own, one, two, three, pick, plain):
    f, _, width = w.shape

    @pl.when(pl.program_id(0) == 0)
    def _():
        pick[...] = picker(W_SUB, [0, 1, 2, 3])

    for j in range(f // W_SUB):
        rows = w[j * W_SUB : (j + 1) * W_SUB].reshape(LAYERS * W_SUB, width)
        got = jnp.dot(pick[...], rows, preferred_element_type=F32).astype(BF)
        for k in range(LAYERS):
            plain[k * f + j * W_SUB : k * f + (j + 1) * W_SUB] = got[k * W_SUB : (k + 1) * W_SUB]

    for place in range(LAYERS):

        @pl.when(idx[0] == place)
        def _():
            rows = plain[: (place + 1) * f]
            terms = lax.dot_general(e[...], rows, (((1,), (1,)), ((), ())), preferred_element_type=F32)
            own[...] = terms[:, :f]
            for k, code in ((1, one), (2, two), (3, three))[:place]:
                encode(terms[:, k * f : (k + 1) * f], code)


def partials(idx, e, decoder):
    tokens, width = e.shape
    f = decoder.shape[0]
    tile = 128
    code = pl.BlockSpec((tokens + SCALE_ROWS, tile), lambda i, s: (0, i))
    return pl.pallas_call(
        partial_kernel,
        name="partials",
        grid_spec=pltpu.PrefetchScalarGridSpec(
            num_scalar_prefetch=1,
            grid=(f // tile,),
            in_specs=[
                pl.BlockSpec((tokens, width), lambda i, s: (0, 0)),
                pl.BlockSpec((tile, LAYERS, width), lambda i, s: (i, 0, 0)),
            ],
            out_specs=[pl.BlockSpec((tokens, tile), lambda i, s: (0, i)), code, code, code],
            scratch_shapes=[
                pltpu.VMEM((LAYERS * W_SUB, LAYERS * W_SUB), BF),
                pltpu.VMEM((LAYERS * tile, width), BF),
            ],
        ),
        out_shape=[jax.ShapeDtypeStruct((tokens, f), F32)] + [jax.ShapeDtypeStruct((tokens + SCALE_ROWS, f), I16)] * 3,
        compiler_params=params(40),
        cost_estimate=cost(8 * tokens * f * width, 20 << 20),
    )(idx, e, decoder)


WEAVE = 64


def weave_kernel(idx, o_keep, o_come, o_scale, b_keep, b_come, b_scale, r_a, r_b, out, mix):
    f, width = o_keep.shape
    place = idx[0]

    @pl.when(pl.program_id(0) == 0)
    def _():
        row = lax.broadcasted_iota(jnp.int32, (LAYERS * WEAVE, LAYERS * WEAVE), 0)
        col = lax.broadcasted_iota(jnp.int32, (LAYERS * WEAVE, LAYERS * WEAVE), 1)
        mix[...] = (col == (row % LAYERS) * WEAVE + row // LAYERS).astype(F32).astype(BF)

    zero = jnp.zeros((WEAVE, width), BF)
    for j in range(f // WEAVE):
        part = slice(j * WEAVE, (j + 1) * WEAVE)
        own = (o_keep[part] + wide(o_come[part]) * unit(o_scale[...])).astype(BF)
        slot_b = (b_keep[part] + wide(b_come[part]) * unit(b_scale[...])).astype(BF)
        one = jnp.where(place == 0, zero, jnp.where(place == 3, r_b[part], slot_b))
        two = jnp.where(place >= 2, r_a[part], zero)
        three = jnp.where(place == 3, slot_b, zero)
        rows = jnp.concatenate([own, one, two, three], axis=0)
        out[part] = jnp.dot(mix[...], rows, preferred_element_type=F32).astype(BF).reshape(WEAVE, LAYERS, width)


def weave(idx, o_keep, o_come, b_keep, b_come, r_a, r_b):
    f, width = o_keep.shape
    tile = 256
    block = pl.BlockSpec((tile, width), lambda i, s: (i, 0))
    scale = pl.BlockSpec((SCALE_ROWS, width), lambda i, s: (f // SCALE_ROWS, 0))
    return pl.pallas_call(
        weave_kernel,
        name="weave",
        grid_spec=pltpu.PrefetchScalarGridSpec(
            num_scalar_prefetch=1,
            grid=(f // tile,),
            in_specs=[block, block, scale, block, block, scale, block, block],
            out_specs=pl.BlockSpec((tile, LAYERS, width), lambda i, s: (i, 0, 0)),
            scratch_shapes=[pltpu.VMEM((LAYERS * WEAVE, LAYERS * WEAVE), BF)],
        ),
        out_shape=jax.ShapeDtypeStruct((f, LAYERS, width), BF),
        compiler_params=params(36),
        cost_estimate=cost(2 * f * LAYERS * 256 * width, 8 << 20),
    )(idx, o_keep, o_come, o_come, b_keep, b_come, b_come, r_a, r_b)


def moved(array, group, pairs):
    return lax.ppermute(array, "dst", [(a * group + i, b * group + i) for a, b in pairs for i in range(group)])


def swapped(array):
    return lax.ppermute(array, "tok", [(0, 1), (1, 0)])


def gate_kernel(mask, own, one, two, three, one_scale, two_scale, three_scale, out):
    total = own[...]
    for code, scale in ((one, one_scale), (two, two_scale), (three, three_scale)):
        total = total + wide(code[...]) * unit(scale[...])
    out[...] = mask[...].astype(F32) * total


def gated(mask, own, terms):
    tokens, f = own.shape
    tile = 512
    block = pl.BlockSpec((tile, f), lambda i: (i, 0))
    scale = pl.BlockSpec((SCALE_ROWS, f), lambda i: (tokens // SCALE_ROWS, 0))
    return pl.pallas_call(
        gate_kernel,
        name="gate",
        grid=(tokens // tile,),
        in_specs=[block] * 5 + [scale] * 3,
        out_specs=block,
        out_shape=jax.ShapeDtypeStruct((tokens, f), F32),
        compiler_params=params(30),
        cost_estimate=cost(8 * tokens * f, 9 << 20),
    )(mask, own, *terms, *terms)


def after(array, earlier):
    return lax.optimization_barrier((array, earlier))[0]


def per_device(latents, mask, errors, decoder):
    group = lax.axis_size("dst") // LAYERS
    place = lax.axis_index("dst") // group
    other = jnp.where(place == 0, 2, 3)
    idx = jnp.stack([place, other, lax.axis_index("tok")]).astype(jnp.int32)

    own_e, l_code, a_code, a_keep, o_code, o_keep = first_terms(idx, errors, latents)
    a_come = swapped(a_code)
    o_come = swapped(o_code)
    near = moved(l_code, group, [(0, 1), (1, 2)])
    far = moved(l_code, group, [(0, 3)])

    own_p, one_p, two_p, three_p = partials(idx, own_e, decoder)
    three = moved(three_p, group, [(3, 0)])
    two = moved(two_p, group, [(3, 1), (2, 0)])
    one = moved(one_p, group, [(3, 2), (2, 1), (1, 0)])

    a_done, b_code, b_keep = more_terms(idx, after(near, own_p), far, own_e, a_keep, a_come)
    b_come = swapped(b_code)
    r_a = moved(a_done, group, [(0, 2), (1, 3)])
    r_b = moved(a_done, group, [(2, 3)])

    latent_grad = gated(after(mask, b_code), own_p, (one, two, three))
    decoder_grad = weave(idx, after(o_keep, latent_grad), o_come, b_keep, b_come, r_a, r_b)
    return decoder_grad, latent_grad


def solution(mesh):
    placed = (P("tok", "dst"), P("tok", "dst"), P("tok", None, None), P("dst", None, None))
    return jax.shard_map(
        per_device,
        mesh=mesh,
        in_specs=placed,
        out_specs=(P("dst", None, "tok"), P("tok", "dst")),
        check_vma=False,
    )
```

```python
import jax
import jax.numpy as jnp
from jax import lax
from jax.experimental import pallas as pl
from jax.experimental.pallas import tpu as pltpu
from jax.sharding import PartitionSpec as P


LAYERS = 4
BF = jnp.bfloat16
F32 = jnp.float32
I16 = jnp.int16
SCALE_ROWS = 16


def params(mib=60):
    return pltpu.CompilerParams(vmem_limit_bytes=mib << 20)


def cost(flops, moved):
    return pl.CostEstimate(flops=flops, bytes_accessed=moved, transcendentals=0)


def picker(tokens, layers):
    row = lax.broadcasted_iota(jnp.int32, (len(layers) * tokens, LAYERS * tokens), 0)
    col = lax.broadcasted_iota(jnp.int32, (len(layers) * tokens, LAYERS * tokens), 1)
    hit = None
    for i, layer in enumerate(layers):
        one = (row >= i * tokens) & (row < (i + 1) * tokens) & (col == (row - i * tokens) * LAYERS + layer)
        hit = one if hit is None else hit | one
    return hit.astype(F32).astype(BF)


def split_transposed(block):
    wide = block.T
    high = wide.astype(BF)
    low = (wide - high.astype(F32)).astype(BF)
    return jnp.concatenate([high, low], axis=1)


def encode(values, out):
    rows = values.shape[0]
    top = jnp.maximum(jnp.max(jnp.abs(values), axis=0, keepdims=True), 1e-30)
    power = jnp.ceil(jnp.log2(top))
    coded = jnp.clip(jnp.round(values * jnp.exp2(15 - power)), -32767, 32767)
    out[:rows] = coded.astype(jnp.int32).astype(I16)
    power = jnp.broadcast_to(power, (SCALE_ROWS, values.shape[1]))
    out[rows:] = power.astype(jnp.int32).astype(I16)


def wide(block):
    return block.astype(jnp.int32).astype(F32)


def unit(scales):
    return jnp.exp2(wide(scales)[:1] - 15)


SUB = 64


def first_kernel(idx, er, lat, own_e, l_code, a_code, a_keep, o_code, pick, e_a, a_send, o_send):
    step = pl.program_id(0)
    tokens, _, width = er.shape
    half = width // 2
    last = step == pl.num_programs(0) - 1
    early = idx[0] < LAYERS - 1

    @pl.when(step == 0)
    def _():
        pick[...] = picker(SUB, [idx[0], idx[1]])

    for j in range(tokens // SUB):
        rows = er[j * SUB : (j + 1) * SUB].reshape(LAYERS * SUB, width)
        got = jnp.dot(pick[...], rows, preferred_element_type=F32).astype(BF)
        own_e[j * SUB : (j + 1) * SUB] = got[:SUB]
        e_a[j * SUB : (j + 1) * SUB] = got[SUB:]
    left = split_transposed(lat[pl.ds(pl.multiple_of(step * tokens, tokens), tokens)])
    keep_at = pl.multiple_of(idx[2] * half, half)
    send_at = pl.multiple_of((1 - idx[2]) * half, half)

    def add(out, source, start):
        right = source[:, pl.ds(start, half)]
        term = jnp.dot(left, jnp.concatenate([right, right], axis=0), preferred_element_type=F32)
        out[...] = term + jnp.where(step > 0, out[...], 0.0)

    add(o_send, own_e, send_at)

    @pl.when(early)
    def _():
        add(a_send, e_a, send_at)
        add(a_keep, e_a, keep_at)

    @pl.when(last & early)
    def _():
        encode(a_send[...], a_code)

    @pl.when(last)
    def _():
        encode(o_send[...], o_code)

    @pl.when(last & (idx[0] < 2))
    def _():
        encode(lat[...], l_code)


def first_terms(idx, errors, latents, tile=256):
    tokens, _, width = errors.shape
    f = latents.shape[1]
    half = width // 2
    whole = pl.BlockSpec((f, half), lambda i, s: (0, 0))
    whole_code = pl.BlockSpec((f + SCALE_ROWS, half), lambda i, s: (0, 0))
    shape = jax.ShapeDtypeStruct((f, half), F32)
    code = jax.ShapeDtypeStruct((f + SCALE_ROWS, half), I16)
    return pl.pallas_call(
        first_kernel,
        name="first_terms",
        grid_spec=pltpu.PrefetchScalarGridSpec(
            num_scalar_prefetch=1,
            grid=(tokens // tile,),
            in_specs=[
                pl.BlockSpec((tile, LAYERS, width), lambda i, s: (i, 0, 0)),
                pl.BlockSpec((tokens, f), lambda i, s: (0, 0)),
            ],
            out_specs=[
                pl.BlockSpec((tile, width), lambda i, s: (i, 0)),
                pl.BlockSpec((tokens + SCALE_ROWS, f), lambda i, s: (0, 0)),
                whole_code,
                whole,
                whole_code,
            ],
            scratch_shapes=[
                pltpu.VMEM((2 * SUB, LAYERS * SUB), BF),
                pltpu.VMEM((tile, width), BF),
                pltpu.VMEM((f, half), F32),
                pltpu.VMEM((f, half), F32),
            ],
        ),
        out_shape=[
            jax.ShapeDtypeStruct((tokens, width), BF),
            jax.ShapeDtypeStruct((tokens + SCALE_ROWS, f), I16),
            code,
            shape,
            code,
        ],
        compiler_params=params(38),
        cost_estimate=cost(16 * tokens * f * width, 30 << 20),
    )(idx, errors, latents)


def more_kernel(idx, near, far, e, code, left):
    rows = near.shape[0] - SCALE_ROWS
    late = idx[0] > 0

    @pl.when((pl.program_id(0) == 0) & late)
    def _():
        both = near[...].astype(jnp.int32) + far[...].astype(jnp.int32)
        left[...] = split_transposed(both[:rows].astype(F32) * jnp.exp2(both[rows : rows + 1].astype(F32) - 15))

    @pl.when(late)
    def _():
        right = e[...]
        encode(jnp.dot(left[...], jnp.concatenate([right, right], axis=0), preferred_element_type=F32), code)


def more_terms(idx, near, far, e):
    rows, f = near.shape
    tokens, width = e.shape
    tile = width // 4
    half = width // 2
    return pl.pallas_call(
        more_kernel,
        name="more_terms",
        grid_spec=pltpu.PrefetchScalarGridSpec(
            num_scalar_prefetch=1,
            grid=(2,),
            in_specs=[
                pl.BlockSpec((rows, f), lambda i, s: (0, 0)),
                pl.BlockSpec((rows, f), lambda i, s: (0, 0)),
                pl.BlockSpec((tokens, tile), lambda i, s: (0, i + 2 * (1 - s[2]))),
            ],
            out_specs=[
                pl.BlockSpec((f + SCALE_ROWS, tile), lambda i, s: (0, i)),
                pl.BlockSpec((f, 2 * tokens), lambda i, s: (0, 0)),
            ],
        ),
        out_shape=[
            jax.ShapeDtypeStruct((f + SCALE_ROWS, half), I16),
            jax.ShapeDtypeStruct((f, 2 * tokens), BF),
        ],
        compiler_params=params(26),
        cost_estimate=cost(2 * tokens * f * width, 8 << 20),
    )(idx, near, far, e)


def rest_kernel(idx, lat, b_left, e, w0, o_keep, b_keep, own, o_left):
    step = pl.program_id(0)
    _, tile = o_keep.shape
    half = e.shape[1] // 2

    @pl.when(step == 0)
    def _():
        o_left[...] = split_transposed(lat[...])

    right = e[:, pl.ds(pl.multiple_of(idx[2] * half + step * tile, tile), tile)]
    right = jnp.concatenate([right, right], axis=0)
    o_keep[...] = jnp.dot(o_left[...], right, preferred_element_type=F32)
    b_keep[...] = jnp.dot(b_left[...], right, preferred_element_type=F32)
    own[...] = lax.dot_general(e[...], w0[...], (((1,), (1,)), ((), ())), preferred_element_type=F32)


def rest_terms(idx, latents, b_left, e, w0):
    tokens, f = latents.shape
    width = e.shape[1]
    half = width // 2
    kept = pl.BlockSpec((f, half // 2), lambda i, s: (0, i))
    return pl.pallas_call(
        rest_kernel,
        name="rest_terms",
        grid_spec=pltpu.PrefetchScalarGridSpec(
            num_scalar_prefetch=1,
            grid=(2,),
            in_specs=[
                pl.BlockSpec((tokens, f), lambda i, s: (0, 0)),
                pl.BlockSpec((f, 2 * tokens), lambda i, s: (0, 0)),
                pl.BlockSpec((tokens, width), lambda i, s: (0, 0)),
                pl.BlockSpec((f // 2, width), lambda i, s: (i, 0)),
            ],
            out_specs=[kept, kept, pl.BlockSpec((tokens, f // 2), lambda i, s: (0, i))],
            scratch_shapes=[pltpu.VMEM((f, 2 * tokens), BF)],
        ),
        out_shape=[jax.ShapeDtypeStruct((f, half), F32)] * 2 + [jax.ShapeDtypeStruct((tokens, f), F32)],
        compiler_params=params(40),
        cost_estimate=cost(6 * tokens * f * width, 16 << 20),
    )(idx, latents, b_left, e, w0)


def join_kernel(keep, come, scale, out):
    out[...] = (keep[...] + wide(come[...]) * unit(scale[...])).astype(BF)


def joined(keep, come):
    f, width = keep.shape
    tile = 256
    block = pl.BlockSpec((tile, width), lambda i: (i, 0))
    return pl.pallas_call(
        join_kernel,
        name="join",
        grid=(f // tile,),
        in_specs=[block, block, pl.BlockSpec((SCALE_ROWS, width), lambda i: (f // SCALE_ROWS, 0))],
        out_specs=block,
        out_shape=jax.ShapeDtypeStruct((f, width), BF),
        compiler_params=params(24),
        cost_estimate=cost(4 * f * width, 4 << 20),
    )(keep, come, come)


W_SUB = 64


def partial_kernel(idx, e, w, zero, one, two, three, pick, plain):
    f, _, width = w.shape

    @pl.when(pl.program_id(0) == 0)
    def _():
        pick[...] = picker(W_SUB, [0, 1, 2, 3])

    for j in range(f // W_SUB):
        rows = w[j * W_SUB : (j + 1) * W_SUB].reshape(LAYERS * W_SUB, width)
        got = jnp.dot(pick[...], rows, preferred_element_type=F32).astype(BF)
        zero[j * W_SUB : (j + 1) * W_SUB] = got[:W_SUB]
        for k in range(1, LAYERS):
            plain[(k - 1) * f + j * W_SUB : (k - 1) * f + (j + 1) * W_SUB] = got[k * W_SUB : (k + 1) * W_SUB]

    for place in range(1, LAYERS):

        @pl.when(idx[0] == place)
        def _():
            rows = plain[: place * f]
            terms = lax.dot_general(e[...], rows, (((1,), (1,)), ((), ())), preferred_element_type=F32)
            for k, code in enumerate((one, two, three)[:place]):
                encode(terms[:, k * f : (k + 1) * f], code)


def partials(idx, e, decoder):
    tokens, width = e.shape
    f = decoder.shape[0]
    tile = 256
    code = pl.BlockSpec((tokens + SCALE_ROWS, tile), lambda i, s: (0, i))
    return pl.pallas_call(
        partial_kernel,
        name="partials",
        grid_spec=pltpu.PrefetchScalarGridSpec(
            num_scalar_prefetch=1,
            grid=(f // tile,),
            in_specs=[
                pl.BlockSpec((tokens, width), lambda i, s: (0, 0)),
                pl.BlockSpec((tile, LAYERS, width), lambda i, s: (i, 0, 0)),
            ],
            out_specs=[pl.BlockSpec((tile, width), lambda i, s: (i, 0)), code, code, code],
            scratch_shapes=[
                pltpu.VMEM((LAYERS * W_SUB, LAYERS * W_SUB), BF),
                pltpu.VMEM(((LAYERS - 1) * tile, width), BF),
            ],
        ),
        out_shape=[jax.ShapeDtypeStruct((f, width), BF)] + [jax.ShapeDtypeStruct((tokens + SCALE_ROWS, f), I16)] * 3,
        compiler_params=params(40),
        cost_estimate=cost(8 * tokens * f * width, 20 << 20),
    )(idx, e, decoder)


WEAVE = 64


def weave_kernel(idx, o_keep, o_come, o_scale, b_keep, b_come, b_scale, r_a, r_b, out, mix):
    f, width = o_keep.shape
    place = idx[0]

    @pl.when(pl.program_id(0) == 0)
    def _():
        row = lax.broadcasted_iota(jnp.int32, (LAYERS * WEAVE, LAYERS * WEAVE), 0)
        col = lax.broadcasted_iota(jnp.int32, (LAYERS * WEAVE, LAYERS * WEAVE), 1)
        mix[...] = (col == (row % LAYERS) * WEAVE + row // LAYERS).astype(F32).astype(BF)

    zero = jnp.zeros((WEAVE, width), BF)
    for j in range(f // WEAVE):
        part = slice(j * WEAVE, (j + 1) * WEAVE)
        own = (o_keep[part] + wide(o_come[part]) * unit(o_scale[...])).astype(BF)
        slot_b = (b_keep[part] + wide(b_come[part]) * unit(b_scale[...])).astype(BF)
        one = jnp.where(place == 0, zero, jnp.where(place == 3, r_b[part], slot_b))
        two = jnp.where(place >= 2, r_a[part], zero)
        three = jnp.where(place == 3, slot_b, zero)
        rows = jnp.concatenate([own, one, two, three], axis=0)
        out[part] = jnp.dot(mix[...], rows, preferred_element_type=F32).astype(BF).reshape(WEAVE, LAYERS, width)


def weave(idx, o_keep, o_come, b_keep, b_come, r_a, r_b):
    f, width = o_keep.shape
    tile = 256
    block = pl.BlockSpec((tile, width), lambda i, s: (i, 0))
    scale = pl.BlockSpec((SCALE_ROWS, width), lambda i, s: (f // SCALE_ROWS, 0))
    return pl.pallas_call(
        weave_kernel,
        name="weave",
        grid_spec=pltpu.PrefetchScalarGridSpec(
            num_scalar_prefetch=1,
            grid=(f // tile,),
            in_specs=[block, block, scale, block, block, scale, block, block],
            out_specs=pl.BlockSpec((tile, LAYERS, width), lambda i, s: (i, 0, 0)),
            scratch_shapes=[pltpu.VMEM((LAYERS * WEAVE, LAYERS * WEAVE), BF)],
        ),
        out_shape=jax.ShapeDtypeStruct((f, LAYERS, width), BF),
        compiler_params=params(36),
        cost_estimate=cost(2 * f * LAYERS * 256 * width, 8 << 20),
    )(idx, o_keep, o_come, o_come, b_keep, b_come, b_come, r_a, r_b)


def moved(array, group, pairs):
    return lax.ppermute(array, "dst", [(a * group + i, b * group + i) for a, b in pairs for i in range(group)])


def swapped(array):
    return lax.ppermute(array, "tok", [(0, 1), (1, 0)])


def gate_kernel(mask, own, one, two, three, one_scale, two_scale, three_scale, out):
    total = own[...]
    for code, scale in ((one, one_scale), (two, two_scale), (three, three_scale)):
        total = total + wide(code[...]) * unit(scale[...])
    out[...] = mask[...].astype(F32) * total


def gated(mask, own, terms):
    tokens, f = own.shape
    tile = 512
    block = pl.BlockSpec((tile, f), lambda i: (i, 0))
    scale = pl.BlockSpec((SCALE_ROWS, f), lambda i: (tokens // SCALE_ROWS, 0))
    return pl.pallas_call(
        gate_kernel,
        name="gate",
        grid=(tokens // tile,),
        in_specs=[block] * 5 + [scale] * 3,
        out_specs=block,
        out_shape=jax.ShapeDtypeStruct((tokens, f), F32),
        compiler_params=params(30),
        cost_estimate=cost(8 * tokens * f, 9 << 20),
    )(mask, own, *terms, *terms)


def per_device(latents, mask, errors, decoder):
    group = lax.axis_size("dst") // LAYERS
    place = lax.axis_index("dst") // group
    other = jnp.where(place == 0, 2, 3)
    idx = jnp.stack([place, other, lax.axis_index("tok")]).astype(jnp.int32)

    own_e, l_code, a_code, a_keep, o_code = first_terms(idx, errors, latents)
    a_come = swapped(a_code)
    o_come = swapped(o_code)
    near = moved(l_code, group, [(0, 1), (1, 2)])
    far = moved(l_code, group, [(0, 3)])

    w0, one_p, two_p, three_p = partials(idx, own_e, decoder)
    three = moved(three_p, group, [(3, 0)])
    two = moved(two_p, group, [(3, 1), (2, 0)])
    one = moved(one_p, group, [(3, 2), (2, 1), (1, 0)])

    a_done = joined(a_keep, a_come)
    r_b = moved(a_done, group, [(2, 3)])
    r_a = moved(a_done, group, [(0, 2), (1, 3)])

    b_code, b_left = more_terms(idx, near, far, own_e)
    b_come = swapped(b_code)
    o_keep, b_keep, own_p = rest_terms(idx, latents, b_left, own_e, w0)

    latent_grad = gated(mask, own_p, (one, two, three))
    decoder_grad = weave(idx, o_keep, o_come, b_keep, b_come, r_a, r_b)
    return decoder_grad, latent_grad


def solution(mesh):
    placed = (P("tok", "dst"), P("tok", "dst"), P("tok", None, None), P("dst", None, None))
    return jax.shard_map(
        per_device,
        mesh=mesh,
        in_specs=placed,
        out_specs=(P("dst", None, "tok"), P("tok", "dst")),
        check_vma=False,
    )
```

```python
import jax
import jax.numpy as jnp
from jax import lax
from jax.experimental import pallas as pl
from jax.experimental.pallas import tpu as pltpu
from jax.sharding import PartitionSpec as P


LAYERS = 4
BF = jnp.bfloat16
F32 = jnp.float32
I16 = jnp.int16
SCALE_ROWS = 8


def params(mib=60):
    return pltpu.CompilerParams(vmem_limit_bytes=mib << 20)


def cost(flops, moved):
    return pl.CostEstimate(flops=flops, bytes_accessed=moved, transcendentals=0)


def picker(tokens, layers):
    row = lax.broadcasted_iota(jnp.int32, (len(layers) * tokens, LAYERS * tokens), 0)
    col = lax.broadcasted_iota(jnp.int32, (len(layers) * tokens, LAYERS * tokens), 1)
    hit = None
    for i, layer in enumerate(layers):
        one = (row >= i * tokens) & (row < (i + 1) * tokens) & (col == (row - i * tokens) * LAYERS + layer)
        hit = one if hit is None else hit | one
    return hit.astype(F32).astype(BF)


def split_transposed(block):
    wide = block.T
    high = wide.astype(BF)
    low = (wide - high.astype(F32)).astype(BF)
    return jnp.concatenate([high, low], axis=1)


def encode(values, out):
    rows = values.shape[0]
    top = jnp.maximum(jnp.max(jnp.abs(values), axis=0, keepdims=True), 1e-30)
    power = jnp.ceil(jnp.log2(top))
    coded = jnp.clip(jnp.round(values * jnp.exp2(15 - power)), -32767, 32767)
    out[:rows] = coded.astype(jnp.int32).astype(I16)
    power = jnp.broadcast_to(power, (SCALE_ROWS, values.shape[1]))
    out[rows:] = power.astype(jnp.int32).astype(I16)


def wide(block):
    return block.astype(jnp.int32).astype(F32)


def unit(scales):
    return jnp.exp2(wide(scales)[:1] - 15)


SUB = 64


def first_kernel(idx, er, lat, own_e, e_keep, high, low, l_code, a_code, o_code, pick, e_a, a_send, o_send):
    step = pl.program_id(0)
    tokens, _, width = er.shape
    half = width // 2
    last = step == pl.num_programs(0) - 1
    early = idx[0] < LAYERS - 1

    @pl.when(step == 0)
    def _():
        pick[...] = picker(SUB, [idx[0], idx[1]])

    for j in range(tokens // SUB):
        rows = er[j * SUB : (j + 1) * SUB].reshape(LAYERS * SUB, width)
        got = jnp.dot(pick[...], rows, preferred_element_type=F32).astype(BF)
        own_e[j * SUB : (j + 1) * SUB] = got[:SUB]
        e_a[j * SUB : (j + 1) * SUB] = got[SUB:]
    left = split_transposed(lat[pl.ds(pl.multiple_of(step * tokens, tokens), tokens)])
    high[...] = left[:, :tokens]
    low[...] = left[:, tokens:]
    keep_at = pl.multiple_of(idx[2] * half, half)
    send_at = pl.multiple_of((1 - idx[2]) * half, half)

    def add(out, source, start):
        right = source[:, pl.ds(start, half)]
        term = jnp.dot(left, jnp.concatenate([right, right], axis=0), preferred_element_type=F32)
        out[...] = term + jnp.where(step > 0, out[...], 0.0)

    add(o_send, own_e, send_at)

    @pl.when(early)
    def _():
        add(a_send, e_a, send_at)
        e_keep[...] = e_a[:, pl.ds(keep_at, half)]

    @pl.when(last & early)
    def _():
        encode(a_send[...], a_code)

    @pl.when(last)
    def _():
        encode(o_send[...], o_code)

    @pl.when(last & (idx[0] < 2))
    def _():
        encode(lat[...], l_code)


def first_terms(idx, errors, latents, tile=256):
    tokens, _, width = errors.shape
    f = latents.shape[1]
    half = width // 2
    left = pl.BlockSpec((f, tile), lambda i, s: (0, i))
    whole_code = pl.BlockSpec((f + SCALE_ROWS, half), lambda i, s: (0, 0))
    shape = pltpu.HBM((f, tokens), BF)
    code = jax.ShapeDtypeStruct((f + SCALE_ROWS, half), I16)
    return pl.pallas_call(
        first_kernel,
        name="first_terms",
        grid_spec=pltpu.PrefetchScalarGridSpec(
            num_scalar_prefetch=1,
            grid=(tokens // tile,),
            in_specs=[
                pl.BlockSpec((tile, LAYERS, width), lambda i, s: (i, 0, 0)),
                pl.BlockSpec((tokens, f), lambda i, s: (0, 0)),
            ],
            out_specs=[
                pl.BlockSpec((tile, width), lambda i, s: (i, 0)),
                pl.BlockSpec((tile, half), lambda i, s: (i, 0)),
                left,
                left,
                pl.BlockSpec((tokens + SCALE_ROWS, f), lambda i, s: (0, 0)),
                whole_code,
                whole_code,
            ],
            scratch_shapes=[
                pltpu.VMEM((2 * SUB, LAYERS * SUB), BF),
                pltpu.VMEM((tile, width), BF),
                pltpu.VMEM((f, half), F32),
                pltpu.VMEM((f, half), F32),
            ],
        ),
        out_shape=[
            jax.ShapeDtypeStruct((tokens, width), BF),
            pltpu.HBM((tokens, half), BF),
            shape,
            shape,
            jax.ShapeDtypeStruct((tokens + SCALE_ROWS, f), I16),
            code,
            code,
        ],
        compiler_params=params(38),
        cost_estimate=cost(16 * tokens * f * width, 30 << 20),
    )(idx, errors, latents)


def more_kernel(idx, near, far, e, code, left):
    rows = near.shape[0] - SCALE_ROWS
    late = idx[0] > 0

    @pl.when((pl.program_id(0) == 0) & late)
    def _():
        both = near[...].astype(jnp.int32) + far[...].astype(jnp.int32)
        left[...] = split_transposed(both[:rows].astype(F32) * jnp.exp2(both[rows : rows + 1].astype(F32) - 15))

    @pl.when(late)
    def _():
        right = e[...]
        encode(jnp.dot(left[...], jnp.concatenate([right, right], axis=0), preferred_element_type=F32), code)


def more_terms(idx, near, far, e):
    rows, f = near.shape
    tokens, width = e.shape
    tile = width // 4
    half = width // 2
    return pl.pallas_call(
        more_kernel,
        name="more_terms",
        grid_spec=pltpu.PrefetchScalarGridSpec(
            num_scalar_prefetch=1,
            grid=(2,),
            in_specs=[
                pl.BlockSpec((rows, f), lambda i, s: (0, 0)),
                pl.BlockSpec((rows, f), lambda i, s: (0, 0)),
                pl.BlockSpec((tokens, tile), lambda i, s: (0, i + 2 * (1 - s[2]))),
            ],
            out_specs=[
                pl.BlockSpec((f + SCALE_ROWS, tile), lambda i, s: (0, i)),
                pl.BlockSpec((f, 2 * tokens), lambda i, s: (0, 0)),
            ],
        ),
        out_shape=[
            jax.ShapeDtypeStruct((f + SCALE_ROWS, half), I16),
            jax.ShapeDtypeStruct((f, 2 * tokens), BF),
        ],
        compiler_params=params(26),
        cost_estimate=cost(2 * tokens * f * width, 8 << 20),
    )(idx, near, far, e)


def rest_kernel(idx, high, low, b_left, e, w0, o_keep, b_keep, own):
    step = pl.program_id(0)
    _, tile = o_keep.shape
    half = e.shape[1] // 2

    right = e[:, pl.ds(pl.multiple_of(idx[2] * half + step * tile, tile), tile)]
    o_keep[...] = jnp.dot(high[...], right, preferred_element_type=F32) + jnp.dot(low[...], right, preferred_element_type=F32)
    right = jnp.concatenate([right, right], axis=0)
    b_keep[...] = jnp.dot(b_left[...], right, preferred_element_type=F32)
    own[...] = lax.dot_general(e[...], w0[...], (((1,), (1,)), ((), ())), preferred_element_type=F32)


def rest_terms(idx, high, low, b_left, e, w0):
    f, tokens = high.shape
    width = e.shape[1]
    half = width // 2
    whole = pl.BlockSpec((f, tokens), lambda i, s: (0, 0))
    kept = pl.BlockSpec((f, half // 2), lambda i, s: (0, i))
    return pl.pallas_call(
        rest_kernel,
        name="rest_terms",
        grid_spec=pltpu.PrefetchScalarGridSpec(
            num_scalar_prefetch=1,
            grid=(2,),
            in_specs=[
                whole,
                whole,
                pl.BlockSpec((f, 2 * tokens), lambda i, s: (0, 0)),
                pl.BlockSpec((tokens, width), lambda i, s: (0, 0)),
                pl.BlockSpec((f // 2, width), lambda i, s: (i, 0)),
            ],
            out_specs=[kept, kept, pl.BlockSpec((tokens, f // 2), lambda i, s: (0, i))],
        ),
        out_shape=[jax.ShapeDtypeStruct((f, half), F32)] * 2 + [jax.ShapeDtypeStruct((tokens, f), F32)],
        compiler_params=params(40),
        cost_estimate=cost(6 * tokens * f * width, 16 << 20),
    )(idx, high, low, b_left, e, w0)


def join_kernel(idx, high, low, e, come, scale, out):
    @pl.when(idx[0] < LAYERS - 1)
    def _():
        right = e[...]
        keep = jnp.dot(high[...], right, preferred_element_type=F32) + jnp.dot(low[...], right, preferred_element_type=F32)
        out[...] = (keep + wide(come[...]) * unit(scale[...])).astype(BF)


def joined(idx, high, low, e, come):
    f, tokens = high.shape
    width = e.shape[1]
    tile = width // 2
    whole = pl.BlockSpec((f, tokens), lambda i, s: (0, 0))
    block = pl.BlockSpec((f, tile), lambda i, s: (0, i))
    return pl.pallas_call(
        join_kernel,
        name="join",
        grid_spec=pltpu.PrefetchScalarGridSpec(
            num_scalar_prefetch=1,
            grid=(2,),
            in_specs=[
                whole,
                whole,
                pl.BlockSpec((tokens, tile), lambda i, s: (0, i)),
                block,
                pl.BlockSpec((SCALE_ROWS, tile), lambda i, s: (f // SCALE_ROWS, i)),
            ],
            out_specs=block,
        ),
        out_shape=jax.ShapeDtypeStruct((f, width), BF),
        compiler_params=params(24),
        cost_estimate=cost(4 * tokens * f * width, 6 << 20),
    )(idx, high, low, e, come, come)


W_SUB = 64


def partial_kernel(idx, e, w, zero, one, two, three, pick, plain):
    f, _, width = w.shape

    @pl.when(pl.program_id(0) == 0)
    def _():
        pick[...] = picker(W_SUB, [0, 1, 2, 3])

    for j in range(f // W_SUB):
        rows = w[j * W_SUB : (j + 1) * W_SUB].reshape(LAYERS * W_SUB, width)
        got = jnp.dot(pick[...], rows, preferred_element_type=F32).astype(BF)
        zero[j * W_SUB : (j + 1) * W_SUB] = got[:W_SUB]
        for k in range(1, LAYERS):
            plain[(k - 1) * f + j * W_SUB : (k - 1) * f + (j + 1) * W_SUB] = got[k * W_SUB : (k + 1) * W_SUB]

    for place in range(1, LAYERS):

        @pl.when(idx[0] == place)
        def _():
            rows = plain[: place * f]
            terms = lax.dot_general(e[...], rows, (((1,), (1,)), ((), ())), preferred_element_type=F32)
            for k, code in enumerate((one, two, three)[:place]):
                encode(terms[:, k * f : (k + 1) * f], code)


def partials(idx, e, decoder):
    tokens, width = e.shape
    f = decoder.shape[0]
    tile = 256
    code = pl.BlockSpec((tokens + SCALE_ROWS, tile), lambda i, s: (0, i))
    return pl.pallas_call(
        partial_kernel,
        name="partials",
        grid_spec=pltpu.PrefetchScalarGridSpec(
            num_scalar_prefetch=1,
            grid=(f // tile,),
            in_specs=[
                pl.BlockSpec((tokens, width), lambda i, s: (0, 0)),
                pl.BlockSpec((tile, LAYERS, width), lambda i, s: (i, 0, 0)),
            ],
            out_specs=[pl.BlockSpec((tile, width), lambda i, s: (i, 0)), code, code, code],
            scratch_shapes=[
                pltpu.VMEM((LAYERS * W_SUB, LAYERS * W_SUB), BF),
                pltpu.VMEM(((LAYERS - 1) * tile, width), BF),
            ],
        ),
        out_shape=[pltpu.HBM((f, width), BF)] + [jax.ShapeDtypeStruct((tokens + SCALE_ROWS, f), I16)] * 3,
        compiler_params=params(40),
        cost_estimate=cost(8 * tokens * f * width, 20 << 20),
    )(idx, e, decoder)


WEAVE = 64


def weave_kernel(idx, o_keep, o_come, o_scale, b_keep, b_come, b_scale, r_a, r_b, out, mix):
    f, width = o_keep.shape
    place = idx[0]

    @pl.when(pl.program_id(0) == 0)
    def _():
        row = lax.broadcasted_iota(jnp.int32, (LAYERS * WEAVE, LAYERS * WEAVE), 0)
        col = lax.broadcasted_iota(jnp.int32, (LAYERS * WEAVE, LAYERS * WEAVE), 1)
        mix[...] = (col == (row % LAYERS) * WEAVE + row // LAYERS).astype(F32).astype(BF)

    zero = jnp.zeros((WEAVE, width), BF)
    for j in range(f // WEAVE):
        part = slice(j * WEAVE, (j + 1) * WEAVE)
        own = (o_keep[part] + wide(o_come[part]) * unit(o_scale[...])).astype(BF)
        slot_b = (b_keep[part] + wide(b_come[part]) * unit(b_scale[...])).astype(BF)
        one = jnp.where(place == 0, zero, jnp.where(place == 3, r_b[part], slot_b))
        two = jnp.where(place >= 2, r_a[part], zero)
        three = jnp.where(place == 3, slot_b, zero)
        rows = jnp.concatenate([own, one, two, three], axis=0)
        out[part] = jnp.dot(mix[...], rows, preferred_element_type=F32).astype(BF).reshape(WEAVE, LAYERS, width)


def weave(idx, o_keep, o_come, b_keep, b_come, r_a, r_b):
    f, width = o_keep.shape
    tile = 256
    block = pl.BlockSpec((tile, width), lambda i, s: (i, 0))
    scale = pl.BlockSpec((SCALE_ROWS, width), lambda i, s: (f // SCALE_ROWS, 0))
    return pl.pallas_call(
        weave_kernel,
        name="weave",
        grid_spec=pltpu.PrefetchScalarGridSpec(
            num_scalar_prefetch=1,
            grid=(f // tile,),
            in_specs=[block, block, scale, block, block, scale, block, block],
            out_specs=pl.BlockSpec((tile, LAYERS, width), lambda i, s: (i, 0, 0)),
            scratch_shapes=[pltpu.VMEM((LAYERS * WEAVE, LAYERS * WEAVE), BF)],
        ),
        out_shape=jax.ShapeDtypeStruct((f, LAYERS, width), BF),
        compiler_params=params(36),
        cost_estimate=cost(2 * f * LAYERS * 256 * width, 8 << 20),
    )(idx, o_keep, o_come, o_come, b_keep, b_come, b_come, r_a, r_b)


def moved(array, group, pairs):
    return lax.ppermute(array, "dst", [(a * group + i, b * group + i) for a, b in pairs for i in range(group)])


def swapped(array):
    return lax.ppermute(array, "tok", [(0, 1), (1, 0)])


def gate_kernel(mask, own, one, two, three, one_scale, two_scale, three_scale, out):
    total = own[...]
    for code, scale in ((one, one_scale), (two, two_scale), (three, three_scale)):
        total = total + wide(code[...]) * unit(scale[...])
    out[...] = mask[...].astype(F32) * total


def gated(mask, own, terms):
    tokens, f = own.shape
    tile = 512
    block = pl.BlockSpec((tile, f), lambda i: (i, 0))
    scale = pl.BlockSpec((SCALE_ROWS, f), lambda i: (tokens // SCALE_ROWS, 0))
    return pl.pallas_call(
        gate_kernel,
        name="gate",
        grid=(tokens // tile,),
        in_specs=[block] * 5 + [scale] * 3,
        out_specs=block,
        out_shape=jax.ShapeDtypeStruct((tokens, f), F32),
        compiler_params=params(30),
        cost_estimate=cost(8 * tokens * f, 9 << 20),
    )(mask, own, *terms, *terms)


def per_device(latents, mask, errors, decoder):
    group = lax.axis_size("dst") // LAYERS
    place = lax.axis_index("dst") // group
    other = jnp.where(place == 0, 2, 3)
    idx = jnp.stack([place, other, lax.axis_index("tok")]).astype(jnp.int32)

    own_e, e_keep, high, low, l_code, a_code, o_code = first_terms(idx, errors, pltpu.with_memory_space_constraint(latents, pltpu.HBM))
    a_come = swapped(a_code)
    o_come = swapped(o_code)
    near = moved(l_code, group, [(0, 1), (1, 2)])
    far = moved(l_code, group, [(0, 3)])

    w0, one_p, two_p, three_p = partials(idx, own_e, decoder)
    three = moved(three_p, group, [(3, 0)])
    two = moved(two_p, group, [(3, 1), (2, 0)])
    one = moved(one_p, group, [(3, 2), (2, 1), (1, 0)])

    a_done = joined(idx, high, low, e_keep, a_come)
    r_b = moved(a_done, group, [(2, 3)])
    r_a = moved(a_done, group, [(0, 2), (1, 3)])

    b_code, b_left = more_terms(idx, near, far, own_e)
    b_come = swapped(b_code)
    o_keep, b_keep, own_p = rest_terms(idx, high, low, b_left, own_e, w0)

    latent_grad = gated(mask, own_p, (one, two, three))
    decoder_grad = weave(idx, o_keep, o_come, b_keep, b_come, r_a, r_b)
    return decoder_grad, latent_grad


def solution(mesh):
    placed = (P("tok", "dst"), P("tok", "dst"), P("tok", None, None), P("dst", None, None))
    return jax.shard_map(
        per_device,
        mesh=mesh,
        in_specs=placed,
        out_specs=(P("dst", None, "tok"), P("tok", "dst")),
        check_vma=False,
    )
```

```python
import jax
import jax.numpy as jnp
from jax import lax
from jax.experimental import pallas as pl
from jax.experimental.pallas import tpu as pltpu
from jax.sharding import PartitionSpec as P


LAYERS = 4
BF = jnp.bfloat16
F32 = jnp.float32
I16 = jnp.int16
SCALE_ROWS = 8


def params(mib=60):
    return pltpu.CompilerParams(vmem_limit_bytes=mib << 20)


def cost(flops, moved):
    return pl.CostEstimate(flops=flops, bytes_accessed=moved, transcendentals=0)


def picker(tokens, layers):
    row = lax.broadcasted_iota(jnp.int32, (len(layers) * tokens, LAYERS * tokens), 0)
    col = lax.broadcasted_iota(jnp.int32, (len(layers) * tokens, LAYERS * tokens), 1)
    hit = None
    for i, layer in enumerate(layers):
        one = (row >= i * tokens) & (row < (i + 1) * tokens) & (col == (row - i * tokens) * LAYERS + layer)
        hit = one if hit is None else hit | one
    return hit.astype(F32).astype(BF)


def split_transposed(block):
    wide = block.T
    high = wide.astype(BF)
    low = (wide - high.astype(F32)).astype(BF)
    return jnp.concatenate([high, low], axis=1)


def encode(values, out):
    rows = values.shape[0]
    top = jnp.maximum(jnp.max(jnp.abs(values), axis=0, keepdims=True), 1e-30)
    power = jnp.ceil(jnp.log2(top))
    coded = jnp.clip(jnp.round(values * jnp.exp2(15 - power)), -32767, 32767)
    out[:rows] = coded.astype(jnp.int32).astype(I16)
    power = jnp.broadcast_to(power, (SCALE_ROWS, values.shape[1]))
    out[rows:] = power.astype(jnp.int32).astype(I16)


def wide(block):
    return block.astype(jnp.int32).astype(F32)


def unit(scales):
    return jnp.exp2(wide(scales)[:1] - 15)


SUB = 64


def first_kernel(idx, er, lat, own_e, e_keep, high, low, l_code, a_code, pick, e_a, a_send):
    step = pl.program_id(0)
    tokens, _, width = er.shape
    half = width // 2
    last = step == pl.num_programs(0) - 1
    early = idx[0] < LAYERS - 1

    @pl.when(step == 0)
    def _():
        pick[...] = picker(SUB, [idx[0], idx[1]])

    for j in range(tokens // SUB):
        rows = er[j * SUB : (j + 1) * SUB].reshape(LAYERS * SUB, width)
        got = jnp.dot(pick[...], rows, preferred_element_type=F32).astype(BF)
        own_e[j * SUB : (j + 1) * SUB] = got[:SUB]
        e_a[j * SUB : (j + 1) * SUB] = got[SUB:]
    left = split_transposed(lat[pl.ds(pl.multiple_of(step * tokens, tokens), tokens)])
    high[...] = left[:, :tokens]
    low[...] = left[:, tokens:]
    keep_at = pl.multiple_of(idx[2] * half, half)
    send_at = pl.multiple_of((1 - idx[2]) * half, half)

    def add(out, source, start):
        right = source[:, pl.ds(start, half)]
        term = jnp.dot(left, jnp.concatenate([right, right], axis=0), preferred_element_type=F32)
        out[...] = term + jnp.where(step > 0, out[...], 0.0)


    @pl.when(early)
    def _():
        add(a_send, e_a, send_at)
        e_keep[...] = e_a[:, pl.ds(keep_at, half)]

    @pl.when(last & early)
    def _():
        encode(a_send[...], a_code)

    @pl.when(last & (idx[0] < 2))
    def _():
        encode(lat[...], l_code)


def first_terms(idx, errors, latents, tile=256):
    tokens, _, width = errors.shape
    f = latents.shape[1]
    half = width // 2
    left = pl.BlockSpec((f, tile), lambda i, s: (0, i))
    whole_code = pl.BlockSpec((f + SCALE_ROWS, half), lambda i, s: (0, 0))
    shape = pltpu.HBM((f, tokens), BF)
    code = jax.ShapeDtypeStruct((f + SCALE_ROWS, half), I16)
    return pl.pallas_call(
        first_kernel,
        name="first_terms",
        grid_spec=pltpu.PrefetchScalarGridSpec(
            num_scalar_prefetch=1,
            grid=(tokens // tile,),
            in_specs=[
                pl.BlockSpec((tile, LAYERS, width), lambda i, s: (i, 0, 0)),
                pl.BlockSpec((tokens, f), lambda i, s: (0, 0)),
            ],
            out_specs=[
                pl.BlockSpec((tile, width), lambda i, s: (i, 0)),
                pl.BlockSpec((tile, half), lambda i, s: (i, 0)),
                left,
                left,
                pl.BlockSpec((tokens + SCALE_ROWS, f), lambda i, s: (0, 0)),
                whole_code,
            ],
            scratch_shapes=[
                pltpu.VMEM((2 * SUB, LAYERS * SUB), BF),
                pltpu.VMEM((tile, width), BF),
                pltpu.VMEM((f, half), F32),
            ],
        ),
        out_shape=[
            jax.ShapeDtypeStruct((tokens, width), BF),
            pltpu.HBM((tokens, half), BF),
            shape,
            shape,
            jax.ShapeDtypeStruct((tokens + SCALE_ROWS, f), I16),
            code,
        ],
        compiler_params=params(38),
        cost_estimate=cost(16 * tokens * f * width, 30 << 20),
    )(idx, errors, latents)


def own_kernel(idx, high, low, e, code):
    right = e[...]
    encode(jnp.dot(high[...], right, preferred_element_type=F32) + jnp.dot(low[...], right, preferred_element_type=F32), code)


def own_terms(idx, high, low, e):
    f, tokens = high.shape
    half = e.shape[1] // 2
    tile = half // 2
    whole = pl.BlockSpec((f, tokens), lambda i, s: (0, 0))
    return pl.pallas_call(
        own_kernel,
        name="own_terms",
        grid_spec=pltpu.PrefetchScalarGridSpec(
            num_scalar_prefetch=1,
            grid=(2,),
            in_specs=[whole, whole, pl.BlockSpec((tokens, tile), lambda i, s: (0, i + 2 * (1 - s[2])))],
            out_specs=pl.BlockSpec((f + SCALE_ROWS, tile), lambda i, s: (0, i)),
        ),
        out_shape=jax.ShapeDtypeStruct((f + SCALE_ROWS, half), I16),
        compiler_params=params(24),
        cost_estimate=cost(4 * tokens * f * half, 6 << 20),
    )(idx, high, low, e)


def more_kernel(idx, near, far, e, code, left):
    rows = near.shape[0] - SCALE_ROWS
    late = idx[0] > 0

    @pl.when((pl.program_id(0) == 0) & late)
    def _():
        both = near[...].astype(jnp.int32) + far[...].astype(jnp.int32)
        left[...] = split_transposed(both[:rows].astype(F32) * jnp.exp2(both[rows : rows + 1].astype(F32) - 15))

    @pl.when(late)
    def _():
        right = e[...]
        encode(jnp.dot(left[...], jnp.concatenate([right, right], axis=0), preferred_element_type=F32), code)


def more_terms(idx, near, far, e):
    rows, f = near.shape
    tokens, width = e.shape
    tile = width // 4
    half = width // 2
    return pl.pallas_call(
        more_kernel,
        name="more_terms",
        grid_spec=pltpu.PrefetchScalarGridSpec(
            num_scalar_prefetch=1,
            grid=(2,),
            in_specs=[
                pl.BlockSpec((rows, f), lambda i, s: (0, 0)),
                pl.BlockSpec((rows, f), lambda i, s: (0, 0)),
                pl.BlockSpec((tokens, tile), lambda i, s: (0, i + 2 * (1 - s[2]))),
            ],
            out_specs=[
                pl.BlockSpec((f + SCALE_ROWS, tile), lambda i, s: (0, i)),
                pl.BlockSpec((f, 2 * tokens), lambda i, s: (0, 0)),
            ],
        ),
        out_shape=[
            jax.ShapeDtypeStruct((f + SCALE_ROWS, half), I16),
            jax.ShapeDtypeStruct((f, 2 * tokens), BF),
        ],
        compiler_params=params(26),
        cost_estimate=cost(2 * tokens * f * width, 8 << 20),
    )(idx, near, far, e)


def rest_kernel(idx, high, low, b_left, e, w0, o_keep, b_keep, own):
    step = pl.program_id(0)
    _, tile = o_keep.shape
    half = e.shape[1] // 2

    right = e[:, pl.ds(pl.multiple_of(idx[2] * half + step * tile, tile), tile)]
    o_keep[...] = jnp.dot(high[...], right, preferred_element_type=F32) + jnp.dot(low[...], right, preferred_element_type=F32)
    right = jnp.concatenate([right, right], axis=0)
    b_keep[...] = jnp.dot(b_left[...], right, preferred_element_type=F32)
    own[...] = lax.dot_general(e[...], w0[...], (((1,), (1,)), ((), ())), preferred_element_type=F32)


def rest_terms(idx, high, low, b_left, e, w0):
    f, tokens = high.shape
    width = e.shape[1]
    half = width // 2
    whole = pl.BlockSpec((f, tokens), lambda i, s: (0, 0))
    kept = pl.BlockSpec((f, half // 2), lambda i, s: (0, i))
    return pl.pallas_call(
        rest_kernel,
        name="rest_terms",
        grid_spec=pltpu.PrefetchScalarGridSpec(
            num_scalar_prefetch=1,
            grid=(2,),
            in_specs=[
                whole,
                whole,
                pl.BlockSpec((f, 2 * tokens), lambda i, s: (0, 0)),
                pl.BlockSpec((tokens, width), lambda i, s: (0, 0)),
                pl.BlockSpec((f // 2, width), lambda i, s: (i, 0)),
            ],
            out_specs=[kept, kept, pl.BlockSpec((tokens, f // 2), lambda i, s: (0, i))],
        ),
        out_shape=[jax.ShapeDtypeStruct((f, half), F32)] * 2 + [jax.ShapeDtypeStruct((tokens, f), F32)],
        compiler_params=params(40),
        cost_estimate=cost(6 * tokens * f * width, 16 << 20),
    )(idx, high, low, b_left, e, w0)


def join_kernel(idx, high, low, e, come, scale, out):
    @pl.when(idx[0] < LAYERS - 1)
    def _():
        right = e[...]
        keep = jnp.dot(high[...], right, preferred_element_type=F32) + jnp.dot(low[...], right, preferred_element_type=F32)
        out[...] = (keep + wide(come[...]) * unit(scale[...])).astype(BF)


def joined(idx, high, low, e, come):
    f, tokens = high.shape
    width = e.shape[1]
    tile = width // 2
    whole = pl.BlockSpec((f, tokens), lambda i, s: (0, 0))
    block = pl.BlockSpec((f, tile), lambda i, s: (0, i))
    return pl.pallas_call(
        join_kernel,
        name="join",
        grid_spec=pltpu.PrefetchScalarGridSpec(
            num_scalar_prefetch=1,
            grid=(2,),
            in_specs=[
                whole,
                whole,
                pl.BlockSpec((tokens, tile), lambda i, s: (0, i)),
                block,
                pl.BlockSpec((SCALE_ROWS, tile), lambda i, s: (f // SCALE_ROWS, i)),
            ],
            out_specs=block,
        ),
        out_shape=jax.ShapeDtypeStruct((f, width), BF),
        compiler_params=params(24),
        cost_estimate=cost(4 * tokens * f * width, 6 << 20),
    )(idx, high, low, e, come, come)


W_SUB = 64


def partial_kernel(idx, e, w, zero, one, two, three, pick, plain):
    f, _, width = w.shape

    @pl.when(pl.program_id(0) == 0)
    def _():
        pick[...] = picker(W_SUB, [0, 1, 2, 3])

    for j in range(f // W_SUB):
        rows = w[j * W_SUB : (j + 1) * W_SUB].reshape(LAYERS * W_SUB, width)
        got = jnp.dot(pick[...], rows, preferred_element_type=F32).astype(BF)
        zero[j * W_SUB : (j + 1) * W_SUB] = got[:W_SUB]
        for k in range(1, LAYERS):
            plain[(k - 1) * f + j * W_SUB : (k - 1) * f + (j + 1) * W_SUB] = got[k * W_SUB : (k + 1) * W_SUB]

    for place in range(1, LAYERS):

        @pl.when(idx[0] == place)
        def _():
            rows = plain[: place * f]
            terms = lax.dot_general(e[...], rows, (((1,), (1,)), ((), ())), preferred_element_type=F32)
            for k, code in enumerate((one, two, three)[:place]):
                encode(terms[:, k * f : (k + 1) * f], code)


def partials(idx, e, decoder):
    tokens, width = e.shape
    f = decoder.shape[0]
    tile = 256
    code = pl.BlockSpec((tokens + SCALE_ROWS, tile), lambda i, s: (0, i))
    return pl.pallas_call(
        partial_kernel,
        name="partials",
        grid_spec=pltpu.PrefetchScalarGridSpec(
            num_scalar_prefetch=1,
            grid=(f // tile,),
            in_specs=[
                pl.BlockSpec((tokens, width), lambda i, s: (0, 0)),
                pl.BlockSpec((tile, LAYERS, width), lambda i, s: (i, 0, 0)),
            ],
            out_specs=[pl.BlockSpec((tile, width), lambda i, s: (i, 0)), code, code, code],
            scratch_shapes=[
                pltpu.VMEM((LAYERS * W_SUB, LAYERS * W_SUB), BF),
                pltpu.VMEM(((LAYERS - 1) * tile, width), BF),
            ],
        ),
        out_shape=[pltpu.HBM((f, width), BF)] + [jax.ShapeDtypeStruct((tokens + SCALE_ROWS, f), I16)] * 3,
        compiler_params=params(40),
        cost_estimate=cost(8 * tokens * f * width, 20 << 20),
    )(idx, e, decoder)


WEAVE = 64


def weave_kernel(idx, o_keep, o_come, o_scale, b_keep, b_come, b_scale, r_a, r_b, out, mix):
    f, width = o_keep.shape
    place = idx[0]

    @pl.when(pl.program_id(0) == 0)
    def _():
        row = lax.broadcasted_iota(jnp.int32, (LAYERS * WEAVE, LAYERS * WEAVE), 0)
        col = lax.broadcasted_iota(jnp.int32, (LAYERS * WEAVE, LAYERS * WEAVE), 1)
        mix[...] = (col == (row % LAYERS) * WEAVE + row // LAYERS).astype(F32).astype(BF)

    zero = jnp.zeros((WEAVE, width), BF)
    for j in range(f // WEAVE):
        part = slice(j * WEAVE, (j + 1) * WEAVE)
        own = (o_keep[part] + wide(o_come[part]) * unit(o_scale[...])).astype(BF)
        slot_b = (b_keep[part] + wide(b_come[part]) * unit(b_scale[...])).astype(BF)
        one = jnp.where(place == 0, zero, jnp.where(place == 3, r_b[part], slot_b))
        two = jnp.where(place >= 2, r_a[part], zero)
        three = jnp.where(place == 3, slot_b, zero)
        rows = jnp.concatenate([own, one, two, three], axis=0)
        out[part] = jnp.dot(mix[...], rows, preferred_element_type=F32).astype(BF).reshape(WEAVE, LAYERS, width)


def weave(idx, o_keep, o_come, b_keep, b_come, r_a, r_b):
    f, width = o_keep.shape
    tile = 256
    block = pl.BlockSpec((tile, width), lambda i, s: (i, 0))
    scale = pl.BlockSpec((SCALE_ROWS, width), lambda i, s: (f // SCALE_ROWS, 0))
    return pl.pallas_call(
        weave_kernel,
        name="weave",
        grid_spec=pltpu.PrefetchScalarGridSpec(
            num_scalar_prefetch=1,
            grid=(f // tile,),
            in_specs=[block, block, scale, block, block, scale, block, block],
            out_specs=pl.BlockSpec((tile, LAYERS, width), lambda i, s: (i, 0, 0)),
            scratch_shapes=[pltpu.VMEM((LAYERS * WEAVE, LAYERS * WEAVE), BF)],
        ),
        out_shape=jax.ShapeDtypeStruct((f, LAYERS, width), BF),
        compiler_params=params(36),
        cost_estimate=cost(2 * f * LAYERS * 256 * width, 8 << 20),
    )(idx, o_keep, o_come, o_come, b_keep, b_come, b_come, r_a, r_b)


def moved(array, group, pairs):
    return lax.ppermute(array, "dst", [(a * group + i, b * group + i) for a, b in pairs for i in range(group)])


def swapped(array):
    return lax.ppermute(array, "tok", [(0, 1), (1, 0)])


def gate_kernel(mask, own, one, two, three, one_scale, two_scale, three_scale, out):
    total = own[...]
    for code, scale in ((one, one_scale), (two, two_scale), (three, three_scale)):
        total = total + wide(code[...]) * unit(scale[...])
    out[...] = mask[...].astype(F32) * total


def gated(mask, own, terms):
    tokens, f = own.shape
    tile = 512
    block = pl.BlockSpec((tile, f), lambda i: (i, 0))
    scale = pl.BlockSpec((SCALE_ROWS, f), lambda i: (tokens // SCALE_ROWS, 0))
    return pl.pallas_call(
        gate_kernel,
        name="gate",
        grid=(tokens // tile,),
        in_specs=[block] * 5 + [scale] * 3,
        out_specs=block,
        out_shape=jax.ShapeDtypeStruct((tokens, f), F32),
        compiler_params=params(30),
        cost_estimate=cost(8 * tokens * f, 9 << 20),
    )(mask, own, *terms, *terms)


def per_device(latents, mask, errors, decoder):
    group = lax.axis_size("dst") // LAYERS
    place = lax.axis_index("dst") // group
    other = jnp.where(place == 0, 2, 3)
    idx = jnp.stack([place, other, lax.axis_index("tok")]).astype(jnp.int32)

    own_e, e_keep, high, low, l_code, a_code = first_terms(idx, errors, pltpu.with_memory_space_constraint(latents, pltpu.HBM))
    a_come = swapped(a_code)
    near = moved(l_code, group, [(0, 1), (1, 2)])
    far = moved(l_code, group, [(0, 3)])

    w0, one_p, two_p, three_p = partials(idx, own_e, decoder)
    three = moved(three_p, group, [(3, 0)])
    two = moved(two_p, group, [(3, 1), (2, 0)])
    o_code = own_terms(idx, high, low, own_e)
    o_come = swapped(o_code)
    one = moved(one_p, group, [(3, 2), (2, 1), (1, 0)])

    a_done = joined(idx, high, low, e_keep, a_come)
    r_b = moved(a_done, group, [(2, 3)])
    r_a = moved(a_done, group, [(0, 2), (1, 3)])

    b_code, b_left = more_terms(idx, near, far, own_e)
    b_come = swapped(b_code)
    o_keep, b_keep, own_p = rest_terms(idx, high, low, b_left, own_e, w0)

    latent_grad = gated(mask, own_p, (one, two, three))
    decoder_grad = weave(idx, o_keep, o_come, b_keep, b_come, r_a, r_b)
    return decoder_grad, latent_grad


def solution(mesh):
    placed = (P("tok", "dst"), P("tok", "dst"), P("tok", None, None), P("dst", None, None))
    return jax.shard_map(
        per_device,
        mesh=mesh,
        in_specs=placed,
        out_specs=(P("dst", None, "tok"), P("tok", "dst")),
        check_vma=False,
    )
```

```python
import jax
import jax.numpy as jnp
from jax import lax
from jax.experimental import pallas as pl
from jax.experimental.pallas import tpu as pltpu
from jax.sharding import PartitionSpec as P


LAYERS = 4
BF = jnp.bfloat16
F32 = jnp.float32
I16 = jnp.int16
SCALE_ROWS = 8


def params(mib=60):
    return pltpu.CompilerParams(vmem_limit_bytes=mib << 20)


def cost(flops, moved):
    return pl.CostEstimate(flops=flops, bytes_accessed=moved, transcendentals=0)


def picker(tokens, layers):
    row = lax.broadcasted_iota(jnp.int32, (len(layers) * tokens, LAYERS * tokens), 0)
    col = lax.broadcasted_iota(jnp.int32, (len(layers) * tokens, LAYERS * tokens), 1)
    hit = None
    for i, layer in enumerate(layers):
        one = (row >= i * tokens) & (row < (i + 1) * tokens) & (col == (row - i * tokens) * LAYERS + layer)
        hit = one if hit is None else hit | one
    return hit.astype(F32).astype(BF)


def split_transposed(block):
    wide = block.T
    high = wide.astype(BF)
    low = (wide - high.astype(F32)).astype(BF)
    return jnp.concatenate([high, low], axis=1)


def encode(values, out):
    rows = values.shape[0]
    top = jnp.maximum(jnp.max(jnp.abs(values), axis=0, keepdims=True), 1e-30)
    power = jnp.ceil(jnp.log2(top))
    coded = jnp.clip(jnp.round(values * jnp.exp2(15 - power)), -32767, 32767)
    out[:rows] = coded.astype(jnp.int32).astype(I16)
    power = jnp.broadcast_to(power, (SCALE_ROWS, values.shape[1]))
    out[rows:] = power.astype(jnp.int32).astype(I16)


def wide(block):
    return block.astype(jnp.int32).astype(F32)


def unit(scales):
    return jnp.exp2(wide(scales)[:1] - 15)


SUB = 64


def first_kernel(idx, er, lat, own_e, e_keep, high, low, l_code, a_code, pick, e_a, a_send):
    step = pl.program_id(0)
    tokens, _, width = er.shape
    half = width // 2
    last = step == pl.num_programs(0) - 1
    early = idx[0] < LAYERS - 1

    @pl.when(step == 0)
    def _():
        pick[...] = picker(SUB, [idx[0], idx[1]])

    for j in range(tokens // SUB):
        rows = er[j * SUB : (j + 1) * SUB].reshape(LAYERS * SUB, width)
        got = jnp.dot(pick[...], rows, preferred_element_type=F32).astype(BF)
        own_e[j * SUB : (j + 1) * SUB] = got[:SUB]
        e_a[j * SUB : (j + 1) * SUB] = got[SUB:]
    left = split_transposed(lat[pl.ds(pl.multiple_of(step * tokens, tokens), tokens)])
    high[...] = left[:, :tokens]
    low[...] = left[:, tokens:]
    keep_at = pl.multiple_of(idx[2] * half, half)
    send_at = pl.multiple_of((1 - idx[2]) * half, half)

    def add(out, source, start):
        right = source[:, pl.ds(start, half)]
        term = jnp.dot(left, jnp.concatenate([right, right], axis=0), preferred_element_type=F32)
        out[...] = term + jnp.where(step > 0, out[...], 0.0)


    @pl.when(early)
    def _():
        add(a_send, e_a, send_at)
        e_keep[...] = e_a[:, pl.ds(keep_at, half)]

    @pl.when(last & early)
    def _():
        encode(a_send[...], a_code)

    @pl.when(last & (idx[0] < 2))
    def _():
        encode(lat[...], l_code)


def first_terms(idx, errors, latents, tile=256):
    tokens, _, width = errors.shape
    f = latents.shape[1]
    half = width // 2
    left = pl.BlockSpec((f, tile), lambda i, s: (0, i))
    whole_code = pl.BlockSpec((f + SCALE_ROWS, half), lambda i, s: (0, 0))
    shape = pltpu.HBM((f, tokens), BF)
    code = jax.ShapeDtypeStruct((f + SCALE_ROWS, half), I16)
    return pl.pallas_call(
        first_kernel,
        name="first_terms",
        grid_spec=pltpu.PrefetchScalarGridSpec(
            num_scalar_prefetch=1,
            grid=(tokens // tile,),
            in_specs=[
                pl.BlockSpec((tile, LAYERS, width), lambda i, s: (i, 0, 0)),
                pl.BlockSpec((tokens, f), lambda i, s: (0, 0)),
            ],
            out_specs=[
                pl.BlockSpec((tile, width), lambda i, s: (i, 0)),
                pl.BlockSpec((tile, half), lambda i, s: (i, 0)),
                left,
                left,
                pl.BlockSpec((tokens + SCALE_ROWS, f), lambda i, s: (0, 0)),
                whole_code,
            ],
            scratch_shapes=[
                pltpu.VMEM((2 * SUB, LAYERS * SUB), BF),
                pltpu.VMEM((tile, width), BF),
                pltpu.VMEM((f, half), F32),
            ],
        ),
        out_shape=[
            jax.ShapeDtypeStruct((tokens, width), BF),
            pltpu.HBM((tokens, half), BF),
            shape,
            shape,
            jax.ShapeDtypeStruct((tokens + SCALE_ROWS, f), I16),
            code,
        ],
        compiler_params=params(38),
        cost_estimate=cost(16 * tokens * f * width, 30 << 20),
    )(idx, errors, latents)


def own_kernel(idx, high, low, e, code):
    right = e[...]
    encode(jnp.dot(high[...], right, preferred_element_type=F32) + jnp.dot(low[...], right, preferred_element_type=F32), code)


def own_terms(idx, high, low, e):
    f, tokens = high.shape
    half = e.shape[1] // 2
    tile = half // 2
    whole = pl.BlockSpec((f, tokens), lambda i, s: (0, 0))
    return pl.pallas_call(
        own_kernel,
        name="own_terms",
        grid_spec=pltpu.PrefetchScalarGridSpec(
            num_scalar_prefetch=1,
            grid=(2,),
            in_specs=[whole, whole, pl.BlockSpec((tokens, tile), lambda i, s: (0, i + 2 * (1 - s[2])))],
            out_specs=pl.BlockSpec((f + SCALE_ROWS, tile), lambda i, s: (0, i)),
        ),
        out_shape=jax.ShapeDtypeStruct((f + SCALE_ROWS, half), I16),
        compiler_params=params(24),
        cost_estimate=cost(4 * tokens * f * half, 6 << 20),
    )(idx, high, low, e)


def more_kernel(idx, near, far, e, code, left):
    rows = near.shape[0] - SCALE_ROWS
    late = idx[0] > 0

    @pl.when((pl.program_id(0) == 0) & late)
    def _():
        both = near[...].astype(jnp.int32) + far[...].astype(jnp.int32)
        left[...] = split_transposed(both[:rows].astype(F32) * jnp.exp2(both[rows : rows + 1].astype(F32) - 15))

    @pl.when(late)
    def _():
        right = e[...]
        encode(jnp.dot(left[...], jnp.concatenate([right, right], axis=0), preferred_element_type=F32), code)


def more_terms(idx, near, far, e):
    rows, f = near.shape
    tokens, width = e.shape
    tile = width // 4
    half = width // 2
    return pl.pallas_call(
        more_kernel,
        name="more_terms",
        grid_spec=pltpu.PrefetchScalarGridSpec(
            num_scalar_prefetch=1,
            grid=(2,),
            in_specs=[
                pl.BlockSpec((rows, f), lambda i, s: (0, 0)),
                pl.BlockSpec((rows, f), lambda i, s: (0, 0)),
                pl.BlockSpec((tokens, tile), lambda i, s: (0, i + 2 * (1 - s[2]))),
            ],
            out_specs=[
                pl.BlockSpec((f + SCALE_ROWS, tile), lambda i, s: (0, i)),
                pl.BlockSpec((f, 2 * tokens), lambda i, s: (0, 0)),
            ],
        ),
        out_shape=[
            jax.ShapeDtypeStruct((f + SCALE_ROWS, half), I16),
            jax.ShapeDtypeStruct((f, 2 * tokens), BF),
        ],
        compiler_params=params(26),
        cost_estimate=cost(2 * tokens * f * width, 8 << 20),
    )(idx, near, far, e)


def rest_kernel(idx, high, low, b_left, e, w0, o_come, o_scale, o_done, b_keep, own):
    step = pl.program_id(0)
    _, tile = o_done.shape
    half = e.shape[1] // 2

    right = e[:, pl.ds(pl.multiple_of(idx[2] * half + step * tile, tile), tile)]
    o_keep = jnp.dot(high[...], right, preferred_element_type=F32) + jnp.dot(low[...], right, preferred_element_type=F32)
    o_done[...] = (o_keep + wide(o_come[...]) * unit(o_scale[...])).astype(BF)
    right = jnp.concatenate([right, right], axis=0)
    b_keep[...] = jnp.dot(b_left[...], right, preferred_element_type=F32)
    own[...] = lax.dot_general(e[...], w0[...], (((1,), (1,)), ((), ())), preferred_element_type=F32)


def rest_terms(idx, high, low, b_left, e, w0, o_come):
    f, tokens = high.shape
    width = e.shape[1]
    half = width // 2
    whole = pl.BlockSpec((f, tokens), lambda i, s: (0, 0))
    kept = pl.BlockSpec((f, half // 2), lambda i, s: (0, i))
    return pl.pallas_call(
        rest_kernel,
        name="rest_terms",
        grid_spec=pltpu.PrefetchScalarGridSpec(
            num_scalar_prefetch=1,
            grid=(2,),
            in_specs=[
                whole,
                whole,
                pl.BlockSpec((f, 2 * tokens), lambda i, s: (0, 0)),
                pl.BlockSpec((tokens, width), lambda i, s: (0, 0)),
                pl.BlockSpec((f // 2, width), lambda i, s: (i, 0)),
                kept,
                pl.BlockSpec((SCALE_ROWS, half // 2), lambda i, s: (f // SCALE_ROWS, i)),
            ],
            out_specs=[kept, kept, pl.BlockSpec((tokens, f // 2), lambda i, s: (0, i))],
        ),
        out_shape=[
            jax.ShapeDtypeStruct((f, half), BF),
            jax.ShapeDtypeStruct((f, half), F32),
            jax.ShapeDtypeStruct((tokens, f), F32),
        ],
        compiler_params=params(40),
        cost_estimate=cost(6 * tokens * f * width, 16 << 20),
    )(idx, high, low, b_left, e, w0, o_come, o_come)


def join_kernel(idx, high, low, e, come, scale, out):
    @pl.when(idx[0] < LAYERS - 1)
    def _():
        right = e[...]
        keep = jnp.dot(high[...], right, preferred_element_type=F32) + jnp.dot(low[...], right, preferred_element_type=F32)
        out[...] = (keep + wide(come[...]) * unit(scale[...])).astype(BF)


def joined(idx, high, low, e, come):
    f, tokens = high.shape
    width = e.shape[1]
    tile = width // 2
    whole = pl.BlockSpec((f, tokens), lambda i, s: (0, 0))
    block = pl.BlockSpec((f, tile), lambda i, s: (0, i))
    return pl.pallas_call(
        join_kernel,
        name="join",
        grid_spec=pltpu.PrefetchScalarGridSpec(
            num_scalar_prefetch=1,
            grid=(2,),
            in_specs=[
                whole,
                whole,
                pl.BlockSpec((tokens, tile), lambda i, s: (0, i)),
                block,
                pl.BlockSpec((SCALE_ROWS, tile), lambda i, s: (f // SCALE_ROWS, i)),
            ],
            out_specs=block,
        ),
        out_shape=jax.ShapeDtypeStruct((f, width), BF),
        compiler_params=params(24),
        cost_estimate=cost(4 * tokens * f * width, 6 << 20),
    )(idx, high, low, e, come, come)


W_SUB = 64


def partial_kernel(idx, e, w, zero, one, two, three, pick, plain):
    f, _, width = w.shape

    @pl.when(pl.program_id(0) == 0)
    def _():
        pick[...] = picker(W_SUB, [0, 1, 2, 3])

    for j in range(f // W_SUB):
        rows = w[j * W_SUB : (j + 1) * W_SUB].reshape(LAYERS * W_SUB, width)
        got = jnp.dot(pick[...], rows, preferred_element_type=F32).astype(BF)
        zero[j * W_SUB : (j + 1) * W_SUB] = got[:W_SUB]
        for k in range(1, LAYERS):
            plain[(k - 1) * f + j * W_SUB : (k - 1) * f + (j + 1) * W_SUB] = got[k * W_SUB : (k + 1) * W_SUB]

    for place in range(1, LAYERS):

        @pl.when(idx[0] == place)
        def _():
            rows = plain[: place * f]
            terms = lax.dot_general(e[...], rows, (((1,), (1,)), ((), ())), preferred_element_type=F32)
            for k, code in enumerate((one, two, three)[:place]):
                encode(terms[:, k * f : (k + 1) * f], code)


def partials(idx, e, decoder):
    tokens, width = e.shape
    f = decoder.shape[0]
    tile = 256
    code = pl.BlockSpec((tokens + SCALE_ROWS, tile), lambda i, s: (0, i))
    return pl.pallas_call(
        partial_kernel,
        name="partials",
        grid_spec=pltpu.PrefetchScalarGridSpec(
            num_scalar_prefetch=1,
            grid=(f // tile,),
            in_specs=[
                pl.BlockSpec((tokens, width), lambda i, s: (0, 0)),
                pl.BlockSpec((tile, LAYERS, width), lambda i, s: (i, 0, 0)),
            ],
            out_specs=[pl.BlockSpec((tile, width), lambda i, s: (i, 0)), code, code, code],
            scratch_shapes=[
                pltpu.VMEM((LAYERS * W_SUB, LAYERS * W_SUB), BF),
                pltpu.VMEM(((LAYERS - 1) * tile, width), BF),
            ],
        ),
        out_shape=[pltpu.HBM((f, width), BF)] + [jax.ShapeDtypeStruct((tokens + SCALE_ROWS, f), I16)] * 3,
        compiler_params=params(40),
        cost_estimate=cost(8 * tokens * f * width, 20 << 20),
    )(idx, e, decoder)


WEAVE = 64


def weave_kernel(idx, o_done, b_keep, b_come, b_scale, r_a, r_b, out, mix):
    f, width = o_done.shape
    place = idx[0]

    @pl.when(pl.program_id(0) == 0)
    def _():
        row = lax.broadcasted_iota(jnp.int32, (LAYERS * WEAVE, LAYERS * WEAVE), 0)
        col = lax.broadcasted_iota(jnp.int32, (LAYERS * WEAVE, LAYERS * WEAVE), 1)
        mix[...] = (col == (row % LAYERS) * WEAVE + row // LAYERS).astype(F32).astype(BF)

    zero = jnp.zeros((WEAVE, width), BF)
    for j in range(f // WEAVE):
        part = slice(j * WEAVE, (j + 1) * WEAVE)
        slot_b = (b_keep[part] + wide(b_come[part]) * unit(b_scale[...])).astype(BF)
        one = jnp.where(place == 0, zero, jnp.where(place == 3, r_b[part], slot_b))
        two = jnp.where(place >= 2, r_a[part], zero)
        three = jnp.where(place == 3, slot_b, zero)
        rows = jnp.concatenate([o_done[part], one, two, three], axis=0)
        out[part] = jnp.dot(mix[...], rows, preferred_element_type=F32).astype(BF).reshape(WEAVE, LAYERS, width)


def weave(idx, o_done, b_keep, b_come, r_a, r_b):
    f, width = o_done.shape
    tile = 512
    block = pl.BlockSpec((tile, width), lambda i, s: (i, 0))
    scale = pl.BlockSpec((SCALE_ROWS, width), lambda i, s: (f // SCALE_ROWS, 0))
    return pl.pallas_call(
        weave_kernel,
        name="weave",
        grid_spec=pltpu.PrefetchScalarGridSpec(
            num_scalar_prefetch=1,
            grid=(f // tile,),
            in_specs=[block, block, block, scale, block, block],
            out_specs=pl.BlockSpec((tile, LAYERS, width), lambda i, s: (i, 0, 0)),
            scratch_shapes=[pltpu.VMEM((LAYERS * WEAVE, LAYERS * WEAVE), BF)],
        ),
        out_shape=jax.ShapeDtypeStruct((f, LAYERS, width), BF),
        compiler_params=params(36),
        cost_estimate=cost(2 * f * LAYERS * 256 * width, 8 << 20),
    )(idx, o_done, b_keep, b_come, b_come, r_a, r_b)


def moved(array, group, pairs):
    return lax.ppermute(array, "dst", [(a * group + i, b * group + i) for a, b in pairs for i in range(group)])


def swapped(array):
    return lax.ppermute(array, "tok", [(0, 1), (1, 0)])


def gate_kernel(mask, own, one, two, three, one_scale, two_scale, three_scale, out):
    total = own[...]
    for code, scale in ((one, one_scale), (two, two_scale), (three, three_scale)):
        total = total + wide(code[...]) * unit(scale[...])
    out[...] = mask[...].astype(F32) * total


def gated(mask, own, terms):
    tokens, f = own.shape
    tile = 512
    block = pl.BlockSpec((tile, f), lambda i: (i, 0))
    scale = pl.BlockSpec((SCALE_ROWS, f), lambda i: (tokens // SCALE_ROWS, 0))
    return pl.pallas_call(
        gate_kernel,
        name="gate",
        grid=(tokens // tile,),
        in_specs=[block] * 5 + [scale] * 3,
        out_specs=block,
        out_shape=jax.ShapeDtypeStruct((tokens, f), F32),
        compiler_params=params(30),
        cost_estimate=cost(8 * tokens * f, 9 << 20),
    )(mask, own, *terms, *terms)


def per_device(latents, mask, errors, decoder):
    group = lax.axis_size("dst") // LAYERS
    place = lax.axis_index("dst") // group
    other = jnp.where(place == 0, 2, 3)
    idx = jnp.stack([place, other, lax.axis_index("tok")]).astype(jnp.int32)

    own_e, e_keep, high, low, l_code, a_code = first_terms(idx, errors, pltpu.with_memory_space_constraint(latents, pltpu.HBM))
    a_come = swapped(a_code)
    near = moved(l_code, group, [(0, 1), (1, 2)])
    far = moved(l_code, group, [(0, 3)])

    w0, one_p, two_p, three_p = partials(idx, own_e, decoder)
    three = moved(three_p, group, [(3, 0)])
    two = moved(two_p, group, [(3, 1), (2, 0)])
    o_code = own_terms(idx, high, low, own_e)
    o_come = swapped(o_code)
    one = moved(one_p, group, [(3, 2), (2, 1), (1, 0)])

    a_done = joined(idx, high, low, e_keep, a_come)
    r_b = moved(a_done, group, [(2, 3)])
    r_a = moved(a_done, group, [(0, 2), (1, 3)])

    b_code, b_left = more_terms(idx, near, far, own_e)
    b_come = swapped(b_code)
    o_done, b_keep, own_p = rest_terms(idx, high, low, b_left, own_e, w0, o_come)

    latent_grad = gated(mask, own_p, (one, two, three))
    decoder_grad = weave(idx, o_done, b_keep, b_come, r_a, r_b)
    return decoder_grad, latent_grad


def solution(mesh):
    placed = (P("tok", "dst"), P("tok", "dst"), P("tok", None, None), P("dst", None, None))
    return jax.shard_map(
        per_device,
        mesh=mesh,
        in_specs=placed,
        out_specs=(P("dst", None, "tok"), P("tok", "dst")),
        check_vma=False,
    )
```
